256 devices in a mesh: rows: 32 (over y, z), mem: 8 (over x, core).
Axes of the slice: x: 4, y: 4, z: 8, core: 2. Of those that a mesh axis runs over, the one named last changes fastest.
Arguments:
- ensemble: float32 [64, 32, 192, 384], P('mem', None, 'rows'), may hold values from 0 to 2
- courant: float32 [3, 32, 192, 384], P(None, None, 'rows'), may hold values from -0.22 to 0.22
- obs_column: int32 [512], P('rows'), may hold values from 0 to 73727, as said below
- obs_value: float32 [32, 512], P(None, 'rows'), may hold values from -6 to 6
- obs_var: float32 [32, 512], P(None, 'rows'), may hold values from 0.5 to 8
Outputs:
- analysis: float32 [64, 32, 192, 384], P('mem', None, 'rows')
The draws below stay inside these ranges and needn't reach their ends.
Inputs may be any that keep to these rules, and one draw needn't show every extreme that they name: `obs_column`: entry p is x * 384 + y with x from (p // 16) * 6 to (p // 16) * 6 + 5.
All inputs are finite; a program needn't handle non-finite values.
Results may differ from the reference program's by a relative error of at most 0.0003.
Values sent between devices are 32-bit elements; how exact they have to be, the bound alone decides.
No kernel may reach another device: no remote copies, remote signals or barrier semaphores. Data moves between devices by JAX's collectives and lax.ppermute only.
A program may use at most 128 MiB of HBM per device.

```python
import math
import jax
import jax.numpy as jnp
from jax import lax

ENSEMBLE_SIZE = 64
VERTICAL_COUNT = 32
ROW_CELLS = 384
RX = 6
PROF_DEV = 16
STEPS = 3
NS_ITERS = 4
GRID_ROWS = 192
NPROF = 512


def draw_obs_column(key, part):
    first_key, second_key = jax.random.split(jax.random.fold_in(key, 11))
    owner = jnp.arange(NPROF, dtype=jnp.int32) // PROF_DEV
    row_offset = jax.random.randint(first_key, (NPROF,), 0, RX, dtype=jnp.int32)
    column_y = jax.random.randint(second_key, (NPROF,), 0, ROW_CELLS, dtype=jnp.int32)
    return ((owner * RX + row_offset) * ROW_CELLS + column_y).astype(jnp.int32)


def block_levels(rng, extent, pieces, low, largest):
    loudness, own = 1.0, jax.random.fold_in(rng, 6)
    for dim, parts in pieces:
        heights = jnp.exp(jax.random.uniform(jax.random.fold_in(own, dim), (parts,), jnp.float32, low / len(pieces), largest / len(pieces)))
        loudness = loudness * jnp.repeat(heights, extent[dim] // parts).reshape([-1 if axis == dim else 1 for axis in range(len(extent))])
    return loudness


def bell_draw(key, extent, spread, limit, cuts=(), held_as=jnp.bfloat16):
    drawn = spread * jax.random.normal(key, extent, jnp.float32)
    if cuts:
        drawn = drawn * block_levels(key, extent, cuts, -0.22, 0.18)
    return jnp.clip(drawn, -limit, limit).astype(held_as)


def setup_inputs(seed: int = 0) -> dict:
    key_list = jax.random.split(jax.random.key(seed), 6)
    ensemble = jnp.clip(2.0 * jax.random.uniform(key_list[0], (ENSEMBLE_SIZE, VERTICAL_COUNT, GRID_ROWS, ROW_CELLS), jnp.float32) ** block_levels(key_list[0], (ENSEMBLE_SIZE, VERTICAL_COUNT, GRID_ROWS, ROW_CELLS), ((0, 8), (2, 32)), -0.2, 0.2), 0.0, 2.0)
    courant = jnp.clip(jax.random.uniform(key_list[1], (3, VERTICAL_COUNT, GRID_ROWS, ROW_CELLS), jnp.float32, -0.22, 0.22) * block_levels(key_list[1], (3, VERTICAL_COUNT, GRID_ROWS, ROW_CELLS), ((2, 32),), -0.4, 0.0), -0.22, 0.22)
    obs_column = draw_obs_column(jax.random.fold_in(key_list[5], 71), 0)
    obs_value = bell_draw(key_list[3], (VERTICAL_COUNT, NPROF), 1.0, 6.0, ((1, 32),), jnp.float32)
    obs_var = jnp.clip(jnp.exp(math.log(8.0) - 2.7725887 * jax.random.uniform(key_list[4], (VERTICAL_COUNT, NPROF), jnp.float32) ** block_levels(key_list[4], (VERTICAL_COUNT, NPROF), ((1, 32),), -0.2, 0.2)), 0.5, 8.0)
    return {"ensemble": ensemble, "courant": courant, "obs_column": obs_column, "obs_value": obs_value, "obs_var": obs_var}


DIFFUSION = 0.05

def advance(padded, courant):
    center = padded[:, :, 1:-1, :]
    below_x = padded[:, :, :-2, :]
    above_x = padded[:, :, 2:, :]
    padded_y = jnp.pad(center, ((0, 0), (0, 0), (0, 0), (1, 1)))
    below_y = padded_y[:, :, :, :-2]
    above_y = padded_y[:, :, :, 2:]
    padded_z = jnp.pad(center, ((0, 0), (1, 1), (0, 0), (0, 0)))
    below_z = padded_z[:, :-2]
    above_z = padded_z[:, 2:]
    change = jnp.zeros_like(center)
    for component, below, above in ((0, below_x, above_x), (1, below_y, above_y), (2, below_z, above_z)):
        velocity = courant[component][None]
        change = change - jnp.maximum(velocity, 0.0) * (center - below) - jnp.minimum(velocity, 0.0) * (above - center) + DIFFUSION * (above + below - 2.0 * center)
    return center + change

def gram_terms(profiles, obs_value, obs_var):
    members_all = profiles.shape[0]
    center = lax.optimization_barrier(jnp.mean(profiles, axis=0))
    scaling = 1.0 / jnp.sqrt((members_all - 1.0) * obs_var)
    scaled = ((profiles - center[None]) * scaling[None]).reshape(members_all, -1)
    innovation = ((obs_value - center) / jnp.sqrt(obs_var)).reshape(-1)
    gram_part = jnp.dot(scaled, scaled.T, precision=lax.Precision.HIGHEST)
    pull_part = jnp.dot(scaled, innovation, precision=lax.Precision.HIGHEST)
    return (gram_part, pull_part)

def mixing(gram_sum, pull_sum):
    members_all = gram_sum.shape[0]
    identity_matrix = jnp.eye(members_all, dtype=jnp.float32)
    system = identity_matrix + gram_sum
    frobenius = jnp.sqrt(jnp.sum(system * system))

    def newton(iteration, carry):
        iterate, inverse_root = carry
        factor = 0.5 * (3.0 * identity_matrix - jnp.dot(inverse_root, iterate, precision=lax.Precision.HIGHEST))
        return (jnp.dot(iterate, factor, precision=lax.Precision.HIGHEST), jnp.dot(factor, inverse_root, precision=lax.Precision.HIGHEST))
    iterate, inverse_root = lax.fori_loop(0, NS_ITERS, newton, (system / frobenius, identity_matrix))
    root_inverse = inverse_root / jnp.sqrt(frobenius)
    mean_shift = jnp.dot(root_inverse, jnp.dot(root_inverse, pull_sum, precision=lax.Precision.HIGHEST), precision=lax.Precision.HIGHEST) / jnp.sqrt(members_all - 1.0)
    centering = identity_matrix - 1.0 / members_all
    return 1.0 / members_all + jnp.dot(centering, mean_shift[:, None] + root_inverse, precision=lax.Precision.HIGHEST)

def reference(ensemble, courant, obs_column, obs_value, obs_var):

    def prior_state(member_index):
        concentration = member_index[None]
        for counter in range(STEPS):
            padded = jnp.pad(concentration, ((0, 0), (0, 0), (1, 1), (0, 0)))
            concentration = advance(padded, courant)
        return concentration[0]
    prior_states = lax.map(prior_state, ensemble)
    state_vectors = prior_states.reshape(ENSEMBLE_SIZE, VERTICAL_COUNT, GRID_ROWS * ROW_CELLS)
    profiles = jnp.take(state_vectors, obs_column, axis=2)
    gram_sum, pull_sum = gram_terms(profiles, obs_value, obs_var)
    transform_weights = mixing(gram_sum, pull_sum)
    updated_ensemble = jnp.dot(transform_weights.T, prior_states.reshape(ENSEMBLE_SIZE, -1), precision=lax.Precision.HIGHEST)
    return updated_ensemble.reshape(ensemble.shape)
```

```python
import functools
import jax
import jax.numpy as jnp
from jax import lax
from jax.experimental import pallas as pl
from jax.experimental.pallas import tpu as pltpu
from jax.sharding import PartitionSpec as P

NS_ITERS = 4
DIFFUSION = 0.05
INTERPRET = False
F32 = jnp.float32
BF16 = jnp.bfloat16
HIGHEST = lax.Precision.HIGHEST
VM = pl.BlockSpec(memory_space=pltpu.VMEM)
SM = pl.BlockSpec(memory_space=pltpu.SMEM)


def call(body, outs, n_in, name, scratch=(), smem=0, flops=0, nbytes=0):
    single = not isinstance(outs, list)
    shapes = [jax.ShapeDtypeStruct(s, F32) for s in (outs if not single else [outs])]
    return pl.pallas_call(
        body,
        out_shape=shapes[0] if single else shapes,
        in_specs=[SM] * smem + [VM] * (n_in - smem),
        out_specs=VM if single else [VM] * len(shapes),
        scratch_shapes=list(scratch),
        cost_estimate=pl.CostEstimate(flops=flops, transcendentals=0, bytes_accessed=nbytes),
        interpret=INTERPRET,
        name=name,
    )


def members_inside(block):
    return jnp.swapaxes(block, 0, 1)


def edges_body(first_ref, last_ref, first_out, last_out):
    for src, dst in ((first_ref, first_out), (last_ref, last_out)):
        for tile in range(src.shape[2] // 8):
            part = pl.ds(8 * tile, 8)
            dst[part] = members_inside(src[:, 0, part, :])


def middle_body(*refs):
    half = len(refs) // 2
    for src, dst in zip(refs[:half], refs[half:]):
        for tile in range(src.shape[2] // 8):
            part = pl.ds(8 * tile, 8)
            dst[part] = members_inside(src[:, 0, part, :])


def fill_coefficients(coef, courant_ref, rows):
    levels, cells = courant_ref.shape[2], courant_ref.shape[3]
    lane = lax.broadcasted_iota(jnp.int32, (levels, cells), 1)
    level = lax.broadcasted_iota(jnp.int32, (levels, cells), 0)
    for slot, row in enumerate(rows):
        total = None
        for d in range(3):
            a = courant_ref[d, row]
            low = jnp.maximum(a, 0.0) + DIFFUSION
            high = DIFFUSION - jnp.minimum(a, 0.0)
            both = low + high
            total = both if total is None else total + both
            if d == 1:
                low = jnp.where(lane == 0, 0.0, low)
                high = jnp.where(lane == cells - 1, 0.0, high)
            if d == 2:
                low = jnp.where(level == 0, 0.0, low)
                high = jnp.where(level == levels - 1, 0.0, high)
            coef[slot, 2 * d] = low
            coef[slot, 2 * d + 1] = high
        coef[slot, 6] = 1.0 - total


def advance_row(dst, below, here, above, coef, slot):
    levels, members, cells = here.shape

    def level_step(z, carry):
        def k(i):
            return jnp.broadcast_to(coef[slot, i, pl.ds(z, 1), :], (members, cells))

        c = here[z]
        new = c * k(6)
        new += k(0) * below[z] + k(1) * above[z]
        new += k(2) * pltpu.roll(c, 1, 1) + k(3) * pltpu.roll(c, cells - 1, 1)
        new += k(4) * here[jnp.maximum(z - 1, 0)] + k(5) * here[jnp.minimum(z + 1, levels - 1)]
        dst[z] = new
        return carry

    lax.fori_loop(0, levels, level_step, 0, unroll=4)


def step1_edges(e0, e1, e4, e5, lo, hi, courant, f0, f5, coef):
    fill_coefficients(coef, courant, (0, 5))
    advance_row(f0, lo, e0, e1, coef, 0)
    advance_row(f5, e4, e5, hi, coef, 1)


def inner_steps(e0, e1, e2, e3, e4, e5, f0, f5, courant, f1, f4, g1, g2, g3, g4, h2, h3, f2, f3, coef):
    fill_coefficients(coef, courant, (1, 2, 3, 4))
    e = [e0, e1, e2, e3, e4, e5]
    f = [f0, f1, f2, f3, f4, f5]
    g = [None, g1, g2, g3, g4]
    for row in (1, 2, 3, 4):
        advance_row(f[row], e[row - 1], e[row], e[row + 1], coef, row - 1)
    for row in (1, 2, 3, 4):
        advance_row(g[row], f[row - 1], f[row], f[row + 1], coef, row - 1)
    for row, h in ((2, h2), (3, h3)):
        advance_row(h, g[row - 1], g[row], g[row + 1], coef, row - 1)


def pair_step(row_a, row_b, ba, ha, aa, bb, hb, ab, courant, outa, outb, coef):
    fill_coefficients(coef, courant, (row_a, row_b))
    advance_row(outa, ba, ha, aa, coef, 0)
    advance_row(outb, bb, hb, ab, coef, 1)


def last_step(info, lo, g0, g1, g4, g5, hi, h1, h2, h3, h4, courant, *rest):
    chunks, prof, full, coef = rest[:8], rest[8], rest[9], rest[10]
    levels, members, cells = g0.shape
    fill_coefficients(coef, courant, (0, 5))
    for row, h in ((1, h1), (2, h2), (3, h3), (4, h4)):
        full[row] = h[...]
    advance_row(full.at[0], lo, g0, g1, coef, 0)
    advance_row(full.at[5], g4, g5, hi, coef, 1)
    per = prof.shape[1] // levels
    lane = lax.broadcasted_iota(jnp.int32, (members, 128), 1)
    group = 128 // per
    acc = [jnp.zeros((members, 128), F32) for _ in range(levels // group)]
    for p in range(per):
        column = jnp.clip(info[1 + p], 0, 6 * cells - 1)
        row = column // cells
        y = column - row * cells
        tile = y // 128
        shift = p - (y - tile * 128) + 128
        for z in range(levels):
            spot = (z % group) * per
            v = full[row, z, :, pl.ds(pl.multiple_of(tile * 128, 128), 128)]
            v = pltpu.roll(v, lax.rem(shift + spot, 128), 1)
            acc[z // group] = jnp.where(lane == spot + p, v, acc[z // group])
    for i, a in enumerate(acc):
        prof[:, pl.ds(128 * i, 128)] = a
    me = info[0]
    depth = levels // 8
    for k in range(8):
        q = lax.bitwise_xor(me, k)
        for row in range(6):
            chunks[k][row] = full[row, pl.ds(q * depth, depth)]


def gram_body(info, own, other, r1, r2, r3, value, var, out, stack, aug):
    me = info[0]
    x, core = lax.div(me, 2), lax.rem(me, 2)
    members = own.shape[0]
    stack[pl.ds(pl.multiple_of(me * members, members), members), :] = own[...]
    stack[pl.ds(pl.multiple_of(lax.bitwise_xor(me, 1) * members, members), members), :] = other[...]
    for k, r in ((1, r1), (2, r2), (3, r3)):
        mate = 2 * lax.bitwise_xor(x, k) + core
        stack[pl.ds(pl.multiple_of(mate * members, members), members), :] = r[pl.ds(0, members), :]
        mate = lax.bitwise_xor(mate, 1)
        stack[pl.ds(pl.multiple_of(mate * members, members), members), :] = r[pl.ds(members, members), :]
    total = stack.shape[0]
    everyone = stack[...]
    center = jnp.sum(everyone, axis=0, keepdims=True) * (1.0 / total)
    scaling = 1.0 / jnp.sqrt((total - 1.0) * var[...])
    scaled = (everyone - center) * scaling
    innovation = (value[...] - center) / jnp.sqrt(var[...])
    aug[pl.ds(0, total), :] = scaled
    first = lax.broadcasted_iota(jnp.int32, everyone.shape, 0) == 0
    aug[pl.ds(total, total), :] = jnp.where(first, jnp.broadcast_to(innovation, everyone.shape), 0.0)
    out[...] = lax.dot_general(
        scaled, aug[...], (((1,), (1,)), ((), ())), precision=HIGHEST, preferred_element_type=F32
    )


def transform_weights(both):
    n = both.shape[0]
    gram = both[:, :n]
    pull = both[:, n:]

    def dot(a, b):
        return jnp.dot(a, b, precision=HIGHEST, preferred_element_type=F32)

    rows = lax.broadcasted_iota(jnp.int32, (n, n), 0)
    cols = lax.broadcasted_iota(jnp.int32, (n, n), 1)
    eye = jnp.where(rows == cols, 1.0, 0.0).astype(F32)
    system = eye + gram
    squares = jnp.sum(jnp.sum(system * system, axis=1, keepdims=True), axis=0, keepdims=True)
    frobenius = jnp.sqrt(squares)
    y = system / frobenius
    z = None
    for i in range(NS_ITERS):
        factor = 0.5 * (3.0 * eye - (y if z is None else dot(z, y)))
        if i < NS_ITERS - 1:
            y = dot(y, factor)
        z = factor if z is None else dot(factor, z)
    root = z / jnp.sqrt(frobenius)
    shift = dot(root, dot(root, pull)) * (1.0 / (n - 1.0) ** 0.5)
    moved = shift[:, :1] + root
    return moved - jnp.sum(moved, axis=0, keepdims=True) * (1.0 / n) + 1.0 / n


def mix_body(info, own, r1, r2, r3, *rest):
    chunks, outs, w_ref, t_ref = rest[:8], rest[8:16], rest[16], rest[17]
    me = info[0]
    weights = transform_weights(own[...] + r1[...] + r2[...] + r3[...])
    n = weights.shape[0]
    w_ref[...] = weights
    for k in range(8):
        q = lax.bitwise_xor(me, k)
        t_ref[pl.ds(8 * k, 8), :] = w_ref[pl.ds(pl.multiple_of(8 * q, 8), 8), :]
    w_ref[...] = t_ref[...].T
    for k in range(8):
        q = lax.bitwise_xor(me, k)
        t_ref[pl.ds(8 * k, 8), :] = w_ref[pl.ds(pl.multiple_of(8 * q, 8), 8), :]
    left = t_ref[...]
    left_hi = left.astype(BF16)
    left_lo = (left - left_hi.astype(F32)).astype(BF16)
    lhs = jnp.concatenate([left_hi, left_lo, left_hi], axis=1)
    rows, depth = chunks[0].shape[0], chunks[0].shape[1]
    for row in range(rows):
        for z in range(depth):
            f = jnp.concatenate([c[row, z] for c in chunks], axis=0)
            hi = f.astype(BF16)
            lo = (f - hi.astype(F32)).astype(BF16)
            o = jnp.dot(lhs, jnp.concatenate([hi, hi, lo], axis=0), preferred_element_type=F32)
            for k in range(8):
                outs[k][row, z] = o[8 * k : 8 * k + 8]


def place_body(info, *rest):
    parts, out, stack = rest[:8], rest[8], rest[9]
    me = info[0]
    depth = parts[0].shape[1]
    for k in range(8):
        q = lax.bitwise_xor(me, k)
        stack[pl.ds(q * depth, depth)] = parts[k][0]
    for tile in range(stack.shape[0] // 8):
        part = pl.ds(8 * tile, 8)
        out[:, 0, part, :] = members_inside(stack[part])


def per_device(ensemble, courant, obs_column, obs_value, obs_var):
    members, levels, rows, cells = ensemble.shape
    count = lax.axis_size("rows")
    mem = lax.axis_size("mem")
    width = rows * cells
    me = lax.axis_index("mem").astype(jnp.int32)
    info = jnp.concatenate([me[None], obs_column - lax.axis_index("rows").astype(jnp.int32) * width])
    field = jnp.transpose(ensemble, (0, 2, 1, 3))
    flow = jnp.transpose(courant, (0, 2, 1, 3))
    row_shape = (levels, members, cells)
    row_bytes = 4 * levels * members * cells
    coef = lambda n: [pltpu.VMEM((n, 7, levels, cells), F32)]

    def row_spec(row):
        return pl.BlockSpec((members, 1, levels, cells), lambda *_: (0, row, 0, 0))

    def relayout(body, which, name):
        full = pl.BlockSpec(row_shape, lambda *_: (0, 0, 0))
        return pl.pallas_call(
            body,
            grid=(1,),
            out_shape=[jax.ShapeDtypeStruct(row_shape, F32)] * len(which),
            in_specs=[row_spec(r) for r in which],
            out_specs=[full] * len(which),
            interpret=INTERPRET,
            name=name,
        )(*([field] * len(which)))

    up = [(i, i + 1) for i in range(count - 1)]
    down = [(i + 1, i) for i in range(count - 1)]

    def exchange(first, last):
        return lax.ppermute(last, "rows", up), lax.ppermute(first, "rows", down)

    e0, e5 = relayout(edges_body, (0, 5), "edge_rows")
    lo, hi = exchange(e0, e5)
    e1, e2, e3, e4 = relayout(middle_body, (1, 2, 3, 4), "middle_rows")
    f0, f5 = call(step1_edges, [row_shape] * 2, 7, "step1_edges", coef(2), nbytes=8 * row_bytes)(
        e0, e1, e4, e5, lo, hi, flow
    )
    lo, hi = exchange(f0, f5)
    f1, f4, g1, g2, g3, g4, h2, h3 = call(
        inner_steps, [row_shape] * 8, 9, "inner_steps",
        [pltpu.VMEM(row_shape, F32)] * 2 + coef(4), nbytes=16 * row_bytes,
    )(e0, e1, e2, e3, e4, e5, f0, f5, flow)
    g0, g5 = call(functools.partial(pair_step, 0, 5), [row_shape] * 2, 7, "step2_edges", coef(2), nbytes=8 * row_bytes)(
        lo, f0, f1, f4, f5, hi, flow
    )
    lo, hi = exchange(g0, g5)
    h1, h4 = call(functools.partial(pair_step, 1, 4), [row_shape] * 2, 7, "step3_inner", coef(2), nbytes=8 * row_bytes)(
        g0, g1, g2, g3, g4, g5, flow
    )
    depth = levels // mem
    chunk_shape = (rows, depth, members, cells)
    obs = obs_value.size
    *chunks, prof = call(
        last_step, [chunk_shape] * 8 + [(members, obs)], 12, "last_step",
        [pltpu.VMEM((rows,) + row_shape, F32)] + coef(2), smem=1, nbytes=20 * row_bytes,
    )(info, lo, g0, g1, g4, g5, hi, h1, h2, h3, h4, flow)

    def swap(a, k):
        return lax.ppermute(a, "mem", [(i, i ^ k) for i in range(mem)])

    other = swap(prof, 1)
    both = jnp.concatenate([prof, other], axis=0)
    far = [swap(both, 2 * k) for k in (1, 2, 3)]
    moved = [chunks[0]] + [swap(chunks[k], k) for k in range(1, 8)]
    part = call(
        gram_body, (8 * members, 16 * members), 8, "gram",
        [pltpu.VMEM((8 * members, obs), F32), pltpu.VMEM((16 * members, obs), F32)], smem=1, nbytes=1 << 18,
    )(info, prof, other, *far, obs_value.reshape(1, obs), obs_var.reshape(1, obs))

    deep = mem
    wide = count // deep
    total = None
    for dy in range(wide):
        pairs = [
            ((y * deep + z) * mem + m, (((y + dy) % wide) * deep + (z + m) % deep) * mem + m)
            for y in range(wide) for z in range(deep) for m in range(mem)
        ]
        got = lax.ppermute(part, ("rows", "mem"), pairs)
        total = got if total is None else total + got
    total = total + swap(total, 1)
    sums = [swap(total, 2 * k) for k in (1, 2, 3)]
    mixed = call(
        mix_body, [chunk_shape] * 8, 13, "mix",
        [pltpu.VMEM((8 * members, 8 * members), F32)] * 2, smem=1, nbytes=12 * row_bytes,
    )(info, total, *sums, *moved)
    back = [mixed[0]] + [swap(mixed[k], k) for k in range(1, 8)]
    part_spec = pl.BlockSpec((1, depth, members, cells), lambda i: (i, 0, 0, 0))
    placed = pl.pallas_call(
        place_body,
        grid=(rows,),
        out_shape=jax.ShapeDtypeStruct((members, rows, levels, cells), F32),
        in_specs=[SM] + [part_spec] * 8,
        out_specs=pl.BlockSpec((members, 1, levels, cells), lambda i: (0, i, 0, 0)),
        scratch_shapes=[pltpu.VMEM(row_shape, F32)],
        interpret=INTERPRET,
        name="place",
    )(info, *back)
    return jnp.transpose(placed, (0, 2, 1, 3))


def solution(mesh):
    return jax.shard_map(
        per_device,
        mesh=mesh,
        in_specs=(
            P("mem", None, "rows", None),
            P(None, None, "rows", None),
            P("rows"),
            P(None, "rows"),
            P(None, "rows"),
        ),
        out_specs=P("mem", None, "rows", None),
        check_vma=False,
    )
```

```python
import functools
import jax
import jax.numpy as jnp
from jax import lax
from jax.experimental import pallas as pl
from jax.experimental.pallas import tpu as pltpu
from jax.sharding import PartitionSpec as P

NS_ITERS = 4
DIFFUSION = 0.05
INTERPRET = False
F32 = jnp.float32
BF16 = jnp.bfloat16
HIGHEST = lax.Precision.HIGHEST
VM = pl.BlockSpec(memory_space=pltpu.VMEM)
SM = pl.BlockSpec(memory_space=pltpu.SMEM)
PARAMS = pltpu.CompilerParams(vmem_limit_bytes=16 * 2**20)
ROUTE = (1, 3, 2)


def call(body, outs, n_in, scratch=(), smem=0, flops=0, nbytes=0):
    single = not isinstance(outs, list)
    shapes = [jax.ShapeDtypeStruct(s, F32) for s in (outs if not single else [outs])]
    return pl.pallas_call(
        body,
        out_shape=shapes[0] if single else shapes,
        in_specs=[SM] * smem + [VM] * (n_in - smem),
        out_specs=VM if single else [VM] * len(shapes),
        scratch_shapes=list(scratch),
        cost_estimate=pl.CostEstimate(flops=flops, transcendentals=0, bytes_accessed=nbytes),
        compiler_params=PARAMS,
        interpret=INTERPRET,
    )


def members_inside(block):
    return jnp.swapaxes(block, 0, 1)


def relayout_row(src, dst):
    for tile in range(src.shape[2] // 8):
        part = pl.ds(8 * tile, 8)
        dst[part] = members_inside(src[:, 0, part, :])


def rows_body(first_ref, last_ref, first_out, last_out):
    relayout_row(first_ref, first_out)
    relayout_row(last_ref, last_out)


def rows_courant_body(first_ref, last_ref, courant, first_out, last_out):
    core = lax.rem(lax.axis_index("mem"), 2)
    levels = first_ref.shape[2]
    for src, dst, row in ((first_ref, first_out, core), (last_ref, last_out, courant.shape[1] - 2 + core)):
        relayout_row(src, dst)
        for d in range(3):
            for tile in range(levels // 8):
                dst[levels + d * (levels // 8) + tile] = courant[d, row, pl.ds(8 * tile, 8), :]


def sum4_body(a, b, c, d, out):
    out[...] = (a[...] + b[...]) + (c[...] + d[...])


def coefficients(coef, slot, tile, levels, speeds, keep=None):
    shape = speeds[0].shape
    lane = lax.broadcasted_iota(jnp.int32, shape, 1)
    level = lax.broadcasted_iota(jnp.int32, shape, 0)
    part = pl.ds(8 * tile, 8)
    total = None
    for d, a in enumerate(speeds):
        low = jnp.maximum(a, 0.0) + DIFFUSION
        high = DIFFUSION - jnp.minimum(a, 0.0)
        both = low + high
        total = both if total is None else total + both
        if d == 1:
            low = jnp.where(lane == 0, 0.0, low)
            high = jnp.where(lane == shape[1] - 1, 0.0, high)
        if d == 2 and tile == 0:
            low = jnp.where(level == 0, 0.0, low)
        if d == 2 and tile == levels // 8 - 1:
            high = jnp.where(level == 7, 0.0, high)
        coef[slot, 2 * d, part] = low if keep is None else low * keep
        coef[slot, 2 * d + 1, part] = high if keep is None else high * keep
    center = 1.0 - total
    coef[slot, 6, part] = center if keep is None else center * keep


def own_coefficients(courant, coef):
    levels = courant.shape[2]
    for row in range(courant.shape[1]):
        for tile in range(levels // 8):
            coefficients(coef, row, tile, levels, [courant[d, row, pl.ds(8 * tile, 8), :] for d in range(3)])


def halo_coefficients(coef, halos):
    core = lax.rem(lax.axis_index("mem"), 2)
    block = lax.axis_index("rows")
    inside = (block > 0, block < lax.axis_size("rows") - 1)
    tiles = halos[0].shape[0] // 11
    levels = 8 * tiles
    for side in range(2):
        keep = jnp.where(inside[side], 1.0, 0.0).astype(F32)
        for part, j in ((halos[2 * side], core), (halos[2 * side + 1], 1 - core)):
            for tile in range(tiles):
                speeds = [part[levels + d * tiles + tile] for d in range(3)]
                coefficients(coef, 2 * side + j, tile, levels, speeds, keep)


def advance_row(dst, below, here, above, coef, slot):
    levels, members, cells = dst.shape

    def level_step(z, carry):
        before, c = carry

        def k(i):
            return jnp.broadcast_to(coef[slot, i, pl.ds(z, 1), :], (members, cells))

        after = here[jnp.minimum(z + 1, levels - 1)]
        new = c * k(6)
        new += k(0) * below[z] + k(1) * above[z]
        new += k(2) * pltpu.roll(c, 1, 1) + k(3) * pltpu.roll(c, cells - 1, 1)
        new += k(4) * before + k(5) * after
        dst[z] = new
        return c, after

    first = here[0]
    lax.fori_loop(0, levels, level_step, (first, first), unroll=32)


def stage_a(lo1, e0, e1, e2, e3, e4, e5, hi1, coef, f0, f1, f4, f5, g1, g2, g3, g4, h2, h3, f2, f3):
    e = [lo1, e0, e1, e2, e3, e4, e5, hi1]
    f = [f0, f1, f2, f3, f4, f5]
    g = [None, g1, g2, g3, g4]
    for row in range(6):
        advance_row(f[row], e[row], e[row + 1], e[row + 2], coef, row)
    for row in (1, 2, 3, 4):
        advance_row(g[row], f[row - 1], f[row], f[row + 1], coef, row)
    for row, h in ((2, h2), (3, h3)):
        advance_row(h, g[row - 1], g[row], g[row + 1], coef, row)


def stage_b(lo2, lo2x, hi2, hi2x, lo1, e0, hi1, e5, f0, f1, f4, f5, g1, g2, g3, g4, coef, *outs):
    fm, fp, g0, g5, h1, h4, side = outs
    halo_coefficients(side, (lo2, lo2x, hi2, hi2x))
    advance_row(fm, lo2, lo1, e0, side, 1)
    advance_row(fp, e5, hi1, hi2, side, 2)
    advance_row(g0, fm, f0, f1, coef, 0)
    advance_row(g5, f4, f5, fp, coef, 5)
    advance_row(h1, g0, g1, g2, coef, 1)
    advance_row(h4, g3, g4, g5, coef, 4)


def stage_c(obs_column, *refs):
    lo3, lo2, lo1, fm, f0, g0, g1, hi3, hi2, hi1, fp, f5, g5, g4, h1, h2, h3, h4, coef, side = refs[:20]
    chunks, prof, one, two, full = refs[20:24], refs[24], refs[25], refs[26], refs[27]
    levels, members, cells = g0.shape
    me = lax.axis_index("mem")
    origin = lax.axis_index("rows") * (6 * cells)
    for row, h in ((1, h1), (2, h2), (3, h3), (4, h4)):
        full[row] = h[...]
    advance_row(one, lo3, lo2, lo1, side, 0)
    advance_row(two, one, fm, f0, side, 1)
    advance_row(full.at[0], two, g0, g1, coef, 0)
    advance_row(one, hi1, hi2, hi3, side, 3)
    advance_row(two, f5, fp, one, side, 2)
    advance_row(full.at[5], g4, g5, two, coef, 5)
    per = prof.shape[1] // levels
    lane = lax.broadcasted_iota(jnp.int32, (members, 128), 1)
    group = 128 // levels
    acc = [jnp.zeros((members, 128), F32) for _ in range(per // group)]
    for p in range(per):
        column = jnp.clip(obs_column[p] - origin, 0, 6 * cells - 1)
        row = lax.div(column, cells)
        y = column - row * cells
        tile = lax.div(y, 128)
        shift = 128 - (y - tile * 128)
        for z in range(levels):
            spot = (p % group) * levels + z
            v = full[row, z, :, pl.ds(pl.multiple_of(tile * 128, 128), 128)]
            v = pltpu.roll(v, lax.rem(shift + spot, 128), 1)
            acc[p // group] = jnp.where(lane == spot, v, acc[p // group])
    for i, a in enumerate(acc):
        prof[:, pl.ds(128 * i, 128)] = a
    depth = levels // 4
    for k in range(4):
        chip = lax.bitwise_xor(lax.div(me, 2), k)
        for row in range(6):
            chunks[k][row] = full[row, pl.ds(chip * depth, depth)]


def flat_rows(ref):
    return jnp.concatenate([ref[pl.ds(p, 1), :] for p in range(ref.shape[0])], axis=1)


def gram_body(*refs):
    profiles, (value, var, out, stack, aug) = refs[:8], refs[8:]
    me = lax.axis_index("mem")
    members = profiles[0].shape[0]
    for k, profile in enumerate(profiles):
        mate = lax.bitwise_xor(me, k)
        stack[pl.ds(pl.multiple_of(mate * members, members), members), :] = profile[...]
    total = stack.shape[0]
    everyone = stack[...]
    center = jnp.sum(everyone, axis=0, keepdims=True) * (1.0 / total)
    variance = flat_rows(var)
    scaling = 1.0 / jnp.sqrt((total - 1.0) * variance)
    scaled = (everyone - center) * scaling
    innovation = (flat_rows(value) - center) / jnp.sqrt(variance)
    aug[pl.ds(0, total), :] = scaled
    first = lax.broadcasted_iota(jnp.int32, everyone.shape, 0) == 0
    aug[pl.ds(total, total), :] = jnp.where(first, jnp.broadcast_to(innovation, everyone.shape), 0.0)
    out[...] = lax.dot_general(
        scaled, aug[...], (((1,), (1,)), ((), ())), precision=HIGHEST, preferred_element_type=F32
    )


def transform_weights(both):
    n = both.shape[0]
    gram = both[:, :n]
    pull = both[:, n:]

    def dot(a, b):
        return jnp.dot(a, b, precision=HIGHEST, preferred_element_type=F32)

    rows = lax.broadcasted_iota(jnp.int32, (n, n), 0)
    cols = lax.broadcasted_iota(jnp.int32, (n, n), 1)
    eye = jnp.where(rows == cols, 1.0, 0.0).astype(F32)
    system = eye + gram
    squares = jnp.sum(jnp.sum(system * system, axis=1, keepdims=True), axis=0, keepdims=True)
    frobenius = jnp.sqrt(squares)
    y = system / frobenius
    z = None
    for i in range(NS_ITERS):
        factor = 0.5 * (3.0 * eye - (y if z is None else dot(z, y)))
        if i < NS_ITERS - 1:
            y = dot(y, factor)
        z = factor if z is None else dot(factor, z)
    root = z / jnp.sqrt(frobenius)
    shift = dot(root, dot(root, pull)) * (1.0 / (n - 1.0) ** 0.5)
    moved = shift[:, :1] + root
    return moved - jnp.sum(moved, axis=0, keepdims=True) * (1.0 / n) + 1.0 / n


def weights_body(own, other, lhs, w_ref, t_ref):
    me = lax.axis_index("mem")
    weights = transform_weights(own[...] + other[...])
    w_ref[...] = weights
    for k in range(8):
        q = lax.bitwise_xor(me, k)
        t_ref[pl.ds(8 * k, 8), :] = w_ref[pl.ds(pl.multiple_of(8 * q, 8), 8), :]
    w_ref[...] = t_ref[...].T
    for k in range(8):
        q = lax.bitwise_xor(me, k)
        t_ref[pl.ds(8 * k, 8), :] = w_ref[pl.ds(pl.multiple_of(8 * q, 8), 8), :]
    left = t_ref[...]
    high = left.astype(BF16).astype(F32)
    lhs[...] = jnp.concatenate([high, left - high, high], axis=1)


def mix_body(left, *rest):
    chunks, outs = rest[:8], rest[8:]
    lhs = left[...].astype(BF16)
    rows, depth = outs[0].shape[1], outs[0].shape[2]
    start = lax.rem(lax.axis_index("mem"), 2) * depth
    for row in range(rows):
        for z in range(depth):
            f = jnp.concatenate([c[row, start + z] for c in chunks], axis=0)
            hi = f.astype(BF16)
            lo = (f - hi.astype(F32)).astype(BF16)
            o = jnp.dot(lhs, jnp.concatenate([hi, hi, lo], axis=0), preferred_element_type=F32)
            for k in range(8):
                outs[k // 2][k % 2, row, z] = o[8 * k : 8 * k + 8]


def place_body(distance, same, cross, *rest):
    out, stack, block, sem = rest[-4:]
    me = lax.axis_index("mem")
    core, chip = lax.rem(me, 2), lax.bitwise_xor(lax.div(me, 2), distance)
    rows, depth = same.shape[1], same.shape[2]
    for row in range(rows):
        stack[pl.ds(core * depth, depth)] = same[0, row]
        stack[pl.ds((1 - core) * depth, depth)] = cross[1, row]
        block[:, row] = members_inside(stack[...])
    levels = pl.ds(pl.multiple_of(chip * 8, 8), 8)
    copy = pltpu.make_async_copy(block, out.at[:, :, levels, :], sem)
    copy.start()
    copy.wait()


def per_device(ensemble, courant, obs_column, obs_value, obs_var):
    members, levels, rows, cells = ensemble.shape
    count = lax.axis_size("rows")
    mem = lax.axis_size("mem")
    field = jnp.transpose(ensemble, (0, 2, 1, 3))
    if not INTERPRET:
        field = pltpu.with_memory_space_constraint(field, pltpu.HBM)
    flow = jnp.transpose(courant, (0, 2, 1, 3))
    row_shape = (levels, members, cells)
    row_bytes = 4 * levels * members * cells

    def row_spec(row):
        return pl.BlockSpec((members, 1, levels, cells), lambda *_: (0, row, 0, 0))

    def relayout(which, with_courant=False):
        full = pl.BlockSpec(row_shape, lambda *_: (0, 0, 0))
        shapes = [jax.ShapeDtypeStruct(row_shape, F32)] * 2
        in_specs, out_specs, args = [row_spec(r) for r in which], [full] * 2, [field, field]
        if with_courant:
            shape = (levels + 3 * levels // 8, members, cells)
            shapes = [jax.ShapeDtypeStruct(shape, F32)] * 2
            in_specs.append(VM)
            out_specs = [pl.BlockSpec(shape, lambda *_: (0, 0, 0))] * 2
            args.append(flow)
        return pl.pallas_call(
            rows_courant_body if with_courant else rows_body,
            grid=(1,),
            out_shape=shapes,
            in_specs=in_specs,
            out_specs=out_specs,
            compiler_params=PARAMS,
            interpret=INTERPRET,
        )(*args)

    up = [(i, i + 1) for i in range(count - 1)]
    down = [(i + 1, i) for i in range(count - 1)]

    def exchange(first, last):
        return lax.ppermute(last, "rows", up), lax.ppermute(first, "rows", down)

    def swap(a, k):
        return lax.ppermute(a, "mem", [(i, i ^ k) for i in range(mem)])

    e0, e5 = relayout((0, 5))
    lo1, hi1 = exchange(e0, e5)
    e1, e4 = relayout((1, 4), True)
    lo2, hi2 = exchange(e1, e4)
    e2, e3 = relayout((2, 3))
    lo3, hi3 = exchange(e2, e3)
    lo2x, hi2x = swap(lo2, 1), swap(hi2, 1)
    coef = call(own_coefficients, (rows, 7, levels, cells), 1, nbytes=7 * row_bytes)(flow)

    f0, f1, f4, f5, g1, g2, g3, g4, h2, h3 = call(
        stage_a, [row_shape] * 10, 9, [pltpu.VMEM(row_shape, F32)] * 2, nbytes=20 * row_bytes,
    )(lo1, e0, e1, e2, e3, e4, e5, hi1, coef)
    fm, fp, g0, g5, h1, h4, side = call(
        stage_b, [row_shape] * 6 + [(4, 7, levels, cells)], 17, nbytes=20 * row_bytes,
    )(lo2, lo2x, hi2, hi2x, lo1, e0, hi1, e5, f0, f1, f4, f5, g1, g2, g3, g4, coef)
    chips = mem // 2
    obs = obs_value.size
    *chunks, prof = call(
        stage_c, [(rows, levels // chips, members, cells)] * chips + [(members, obs)], 21,
        [pltpu.VMEM(row_shape, F32)] * 2 + [pltpu.VMEM((rows,) + row_shape, F32)],
        smem=1, nbytes=30 * row_bytes,
    )(obs_column, lo3, lo2, lo1, fm, f0, g0, g1, hi3, hi2, hi1, fp, f5, g5, g4, h1, h2, h3, h4, coef, side)

    def along_chips(parts):
        got = {0: parts[0]}
        for k in ROUTE:
            got[k] = swap(parts[k], 2 * k)
        return [(got[k], swap(got[k], 1)) for k in (0,) + ROUTE]

    far = [swap(prof, 2 * k) for k in (1, 2, 3)]
    profiles = []
    for a in [prof] + far:
        profiles += [a, swap(a, 1)]
    pairs = dict(zip((0,) + ROUTE, along_chips(chunks)))
    moved = [block for k in range(chips) for block in pairs[k]]
    part = call(
        gram_body, (8 * members, 16 * members), 10,
        [pltpu.VMEM((8 * members, obs), F32), pltpu.VMEM((16 * members, obs), F32)], nbytes=1 << 18,
    )(*profiles, obs_value.T, obs_var.T)

    deep = mem
    wide = count // deep

    def shifted(a, dy, dz):
        pairs = [
            ((y * deep + z) * mem + m, (((y + dy) % wide) * deep + (z + dz[m % 2]) % deep) * mem + m)
            for y in range(wide) for z in range(deep) for m in range(mem)
        ]
        return lax.ppermute(a, ("rows", "mem"), pairs)

    got = [shifted(part, 0, dz) for dz in ((1, -1), (2, -2), (3, -3), (0, 4))]
    sum4 = call(sum4_body, part.shape, 4, nbytes=1 << 17)
    total = sum4(*got)
    if wide == 4:
        total = sum4(total, *[shifted(total, dy, (0, 0)) for dy in range(1, wide)])
    n = 8 * members
    left = call(weights_body, (n, 3 * n), 2, [pltpu.VMEM((n, n), F32)] * 2, nbytes=1 << 17)(total, swap(total, 1))
    mixed = call(mix_body, [(2, rows, levels // mem, members, cells)] * chips, 9, nbytes=18 * row_bytes)(left, *moved)
    placed = None
    shape = (members, rows, levels, cells)
    for k, (same, cross) in zip((0,) + ROUTE, along_chips(mixed)):
        placed = pl.pallas_call(
            functools.partial(place_body, k),
            out_shape=jax.ShapeDtypeStruct(shape, F32),
            in_specs=[VM, VM] + ([] if placed is None else [pl.BlockSpec(memory_space=pl.ANY)]),
            out_specs=pl.BlockSpec(memory_space=pl.ANY),
            scratch_shapes=[
                pltpu.VMEM((8, members, cells), F32),
                pltpu.VMEM((members, rows, 8, cells), F32),
                pltpu.SemaphoreType.DMA,
            ],
            input_output_aliases={} if placed is None else {2: 0},
            compiler_params=PARAMS,
            interpret=INTERPRET,
        )(same, cross, *([] if placed is None else [placed]))
    return jnp.transpose(placed, (0, 2, 1, 3))


def solution(mesh):
    return jax.shard_map(
        per_device,
        mesh=mesh,
        in_specs=(
            P("mem", None, "rows", None),
            P(None, None, "rows", None),
            P("rows"),
            P(None, "rows"),
            P(None, "rows"),
        ),
        out_specs=P("mem", None, "rows", None),
        check_vma=False,
    )
```

```python
import functools
import jax
import jax.numpy as jnp
from jax import lax
from jax.experimental import pallas as pl
from jax.experimental.pallas import tpu as pltpu
from jax.sharding import PartitionSpec as P

NS_ITERS = 4
DIFFUSION = 0.05
INTERPRET = False
F32 = jnp.float32
BF16 = jnp.bfloat16
HIGHEST = lax.Precision.HIGHEST
VM = pl.BlockSpec(memory_space=pltpu.VMEM)
SM = pl.BlockSpec(memory_space=pltpu.SMEM)
PARAMS = pltpu.CompilerParams(vmem_limit_bytes=16 * 2**20)
ROUTE = (1, 3, 2)
OUTER = (0, 1, 4, 5)


def call(body, outs, n_in, scratch=(), smem=0, flops=0, nbytes=0):
    single = not isinstance(outs, list)
    shapes = [jax.ShapeDtypeStruct(s, F32) for s in (outs if not single else [outs])]
    return pl.pallas_call(
        body,
        out_shape=shapes[0] if single else shapes,
        in_specs=[SM] * smem + [VM] * (n_in - smem),
        out_specs=VM if single else [VM] * len(shapes),
        scratch_shapes=list(scratch),
        cost_estimate=pl.CostEstimate(flops=flops, transcendentals=0, bytes_accessed=nbytes),
        compiler_params=PARAMS,
        interpret=INTERPRET,
    )


def members_inside(block):
    return jnp.swapaxes(block, 0, 1)


def relayout_row(src, dst):
    for tile in range(src.shape[2] // 8):
        part = pl.ds(8 * tile, 8)
        dst[part] = members_inside(src[:, 0, part, :])


def rows_body(first_ref, last_ref, first_out, last_out):
    relayout_row(first_ref, first_out)
    relayout_row(last_ref, last_out)


def rows_courant_body(first_ref, last_ref, courant, first_out, last_out):
    core = lax.rem(lax.axis_index("mem"), 2)
    levels = first_ref.shape[2]
    for src, dst, row in ((first_ref, first_out, core), (last_ref, last_out, courant.shape[1] - 2 + core)):
        relayout_row(src, dst)
        for d in range(3):
            for tile in range(levels // 8):
                dst[levels + d * (levels // 8) + tile] = courant[d, row, pl.ds(8 * tile, 8), :]


def pick_body(one, three, out):
    core = lax.rem(lax.axis_index("mem"), 2)
    for value, ref in ((0, one), (1, three)):

        @pl.when(core == value)
        def _():
            out[...] = ref[...]


def sum4_body(a, b, c, d, out):
    out[...] = (a[...] + b[...]) + (c[...] + d[...])


def coefficients(coef, slot, tile, levels, speeds, keep=None):
    shape = speeds[0].shape
    lane = lax.broadcasted_iota(jnp.int32, shape, 1)
    level = lax.broadcasted_iota(jnp.int32, shape, 0)
    part = pl.ds(8 * tile, 8)
    total = None
    for d, a in enumerate(speeds):
        low = jnp.maximum(a, 0.0) + DIFFUSION
        high = DIFFUSION - jnp.minimum(a, 0.0)
        both = low + high
        total = both if total is None else total + both
        if d == 1:
            low = jnp.where(lane == 0, 0.0, low)
            high = jnp.where(lane == shape[1] - 1, 0.0, high)
        if d == 2 and tile == 0:
            low = jnp.where(level == 0, 0.0, low)
        if d == 2 and tile == levels // 8 - 1:
            high = jnp.where(level == 7, 0.0, high)
        coef[slot, 2 * d, part] = low if keep is None else low * keep
        coef[slot, 2 * d + 1, part] = high if keep is None else high * keep
    center = 1.0 - total
    coef[slot, 6, part] = center if keep is None else center * keep


def own_coefficients(courant, coef):
    levels = courant.shape[2]
    for row in range(courant.shape[1]):
        for tile in range(levels // 8):
            coefficients(coef, row, tile, levels, [courant[d, row, pl.ds(8 * tile, 8), :] for d in range(3)])


def halo_coefficients(coef, halos):
    core = lax.rem(lax.axis_index("mem"), 2)
    block = lax.axis_index("rows")
    inside = (block > 0, block < lax.axis_size("rows") - 1)
    tiles = halos[0].shape[0] // 11
    levels = 8 * tiles
    for side in range(2):
        keep = jnp.where(inside[side], 1.0, 0.0).astype(F32)
        for part, j in ((halos[2 * side], core), (halos[2 * side + 1], 1 - core)):
            for tile in range(tiles):
                speeds = [part[levels + d * tiles + tile] for d in range(3)]
                coefficients(coef, 2 * side + j, tile, levels, speeds, keep)


def advance_row(dst, below, here, above, coef, slot):
    levels, members, cells = dst.shape

    def level_step(z, carry):
        before, c = carry

        def k(i):
            return jnp.broadcast_to(coef[slot, i, pl.ds(z, 1), :], (members, cells))

        after = here[jnp.minimum(z + 1, levels - 1)]
        new = c * k(6)
        new += k(0) * below[z] + k(1) * above[z]
        new += k(2) * pltpu.roll(c, 1, 1) + k(3) * pltpu.roll(c, cells - 1, 1)
        new += k(4) * before + k(5) * after
        dst[z] = new
        return c, after

    first = here[0]
    lax.fori_loop(0, levels, level_step, (first, first), unroll=32)


def stage_a(lo1, e0, e1, e2, e3, e4, e5, hi1, coef, f0, f1, f4, f5, g1, g2, g3, g4, h23, f2, f3):
    e = [lo1, e0, e1, e2, e3, e4, e5, hi1]
    f = [f0, f1, f2, f3, f4, f5]
    g = [None, g1, g2, g3, g4]
    for row in range(6):
        advance_row(f[row], e[row], e[row + 1], e[row + 2], coef, row)
    for row in (1, 2, 3, 4):
        advance_row(g[row], f[row - 1], f[row], f[row + 1], coef, row)
    for row in (2, 3):
        advance_row(h23.at[row - 2], g[row - 1], g[row], g[row + 1], coef, row)


def stage_b(lo2, lo2x, hi2, hi2x, lo1, e0, hi1, e5, f0, f1, f4, f5, g1, g2, g3, g4, coef, *outs):
    fm, fp, g0, g5, h1, h4, side = outs
    halo_coefficients(side, (lo2, lo2x, hi2, hi2x))
    advance_row(fm, lo2, lo1, e0, side, 1)
    advance_row(fp, e5, hi1, hi2, side, 2)
    advance_row(g0, fm, f0, f1, coef, 0)
    advance_row(g5, f4, f5, fp, coef, 5)
    advance_row(h1, g0, g1, g2, coef, 1)
    advance_row(h4, g3, g4, g5, coef, 4)


def stage_c(obs_column, *refs):
    lo3, lo2, lo1, fm, f0, g0, g1, hi3, hi2, hi1, fp, f5, g5, g4, h1, h23, h4, coef, side = refs[:19]
    chunks, prof, one, two, full = refs[19:23], refs[23], refs[24], refs[25], refs[26]
    levels, members, cells = g0.shape
    me = lax.axis_index("mem")
    origin = lax.axis_index("rows") * (6 * cells)
    full[1] = h1[...]
    full[pl.ds(2, 2)] = h23[...]
    full[4] = h4[...]
    advance_row(one, lo3, lo2, lo1, side, 0)
    advance_row(two, one, fm, f0, side, 1)
    advance_row(full.at[0], two, g0, g1, coef, 0)
    advance_row(one, hi1, hi2, hi3, side, 3)
    advance_row(two, f5, fp, one, side, 2)
    advance_row(full.at[5], g4, g5, two, coef, 5)
    per = prof.shape[1] // levels
    lane = lax.broadcasted_iota(jnp.int32, (members, 128), 1)
    group = 128 // levels
    acc = [jnp.zeros((members, 128), F32) for _ in range(per // group)]
    for p in range(per):
        column = jnp.clip(obs_column[p] - origin, 0, 6 * cells - 1)
        row = lax.div(column, cells)
        y = column - row * cells
        tile = lax.div(y, 128)
        shift = 128 - (y - tile * 128)
        for z in range(levels):
            spot = (p % group) * levels + z
            v = full[row, z, :, pl.ds(pl.multiple_of(tile * 128, 128), 128)]
            v = pltpu.roll(v, lax.rem(shift + spot, 128), 1)
            acc[p // group] = jnp.where(lane == spot, v, acc[p // group])
    for i, a in enumerate(acc):
        prof[:, pl.ds(128 * i, 128)] = a
    depth = levels // 4
    for k in range(4):
        chip = lax.bitwise_xor(lax.div(me, 2), k)
        for i, row in enumerate(OUTER):
            chunks[k][i] = full[row, pl.ds(chip * depth, depth)]


def flat_rows(ref):
    return jnp.concatenate([ref[pl.ds(p, 1), :] for p in range(ref.shape[0])], axis=1)


def gram_body(*refs):
    profiles, (value, var, out, stack, aug) = refs[:8], refs[8:]
    me = lax.axis_index("mem")
    members = profiles[0].shape[0]
    for k, profile in enumerate(profiles):
        mate = lax.bitwise_xor(me, k)
        stack[pl.ds(pl.multiple_of(mate * members, members), members), :] = profile[...]
    total = stack.shape[0]
    everyone = stack[...]
    center = jnp.sum(everyone, axis=0, keepdims=True) * (1.0 / total)
    variance = flat_rows(var)
    scaling = 1.0 / jnp.sqrt((total - 1.0) * variance)
    scaled = (everyone - center) * scaling
    innovation = (flat_rows(value) - center) / jnp.sqrt(variance)
    aug[pl.ds(0, total), :] = scaled
    first = lax.broadcasted_iota(jnp.int32, everyone.shape, 0) == 0
    aug[pl.ds(total, total), :] = jnp.where(first, jnp.broadcast_to(innovation, everyone.shape), 0.0)
    out[...] = lax.dot_general(
        scaled, aug[...], (((1,), (1,)), ((), ())), precision=HIGHEST, preferred_element_type=F32
    )


def transform_weights(both):
    n = both.shape[0]
    gram = both[:, :n]
    pull = both[:, n:]

    def dot(a, b):
        return jnp.dot(a, b, precision=HIGHEST, preferred_element_type=F32)

    rows = lax.broadcasted_iota(jnp.int32, (n, n), 0)
    cols = lax.broadcasted_iota(jnp.int32, (n, n), 1)
    eye = jnp.where(rows == cols, 1.0, 0.0).astype(F32)
    system = eye + gram
    squares = jnp.sum(jnp.sum(system * system, axis=1, keepdims=True), axis=0, keepdims=True)
    frobenius = jnp.sqrt(squares)
    y = system / frobenius
    z = None
    for i in range(NS_ITERS):
        factor = 0.5 * (3.0 * eye - (y if z is None else dot(z, y)))
        if i < NS_ITERS - 1:
            y = dot(y, factor)
        z = factor if z is None else dot(factor, z)
    root = z / jnp.sqrt(frobenius)
    shift = dot(root, dot(root, pull)) * (1.0 / (n - 1.0) ** 0.5)
    moved = shift[:, :1] + root
    return moved - jnp.sum(moved, axis=0, keepdims=True) * (1.0 / n) + 1.0 / n


def weights_body(own, other, lhs, w_ref, t_ref):
    me = lax.axis_index("mem")
    weights = transform_weights(own[...] + other[...])
    w_ref[...] = weights
    for k in range(8):
        q = lax.bitwise_xor(me, k)
        t_ref[pl.ds(8 * k, 8), :] = w_ref[pl.ds(pl.multiple_of(8 * q, 8), 8), :]
    w_ref[...] = t_ref[...].T
    for k in range(8):
        q = lax.bitwise_xor(me, k)
        t_ref[pl.ds(8 * k, 8), :] = w_ref[pl.ds(pl.multiple_of(8 * q, 8), 8), :]
    left = t_ref[...]
    high = left.astype(BF16).astype(F32)
    lhs[...] = jnp.concatenate([high, left - high, high], axis=1)


def mixed_levels(lhs, blocks):
    f = jnp.concatenate(blocks, axis=0)
    hi = f.astype(BF16)
    lo = (f - hi.astype(F32)).astype(BF16)
    return jnp.dot(lhs, jnp.concatenate([hi, hi, lo], axis=0), preferred_element_type=F32)


def mix_body(left, *rest):
    chunks, outs = rest[:8], rest[8:]
    lhs = left[...].astype(BF16)
    rows, depth = outs[0].shape[1], outs[0].shape[2]
    start = lax.rem(lax.axis_index("mem"), 2) * depth
    for row in range(rows):
        for z in range(depth):
            o = mixed_levels(lhs, [c[row, start + z] for c in chunks])
            for k in range(8):
                outs[k // 2][k % 2, row, z] = o[8 * k : 8 * k + 8]


def inner_body(left, *rest):
    fields, (out, stack, block, sem) = rest[:8], rest[-4:]
    members = stack.shape[1]
    lhs = left[pl.ds(0, 2 * members), :].astype(BF16)
    for row in range(2):

        def tile(t, carry):
            for z in range(8):
                o = mixed_levels(lhs, [f[row, 8 * t + z] for f in fields])
                stack[z] = o[:members]
            block[:, row, pl.ds(pl.multiple_of(8 * t, 8), 8), :] = members_inside(stack[...])
            return carry

        lax.fori_loop(0, fields[0].shape[1] // 8, tile, 0)
    copy = pltpu.make_async_copy(block, out.at[:, pl.ds(2, 2)], sem)
    copy.start()
    copy.wait()


def place_body(distance, same, cross, *rest):
    out, stack, block, sems = rest[-4:]
    me = lax.axis_index("mem")
    core, chip = lax.rem(me, 2), lax.bitwise_xor(lax.div(me, 2), distance)
    rows, depth = same.shape[1], same.shape[2]
    for row in range(rows):
        stack[pl.ds(core * depth, depth)] = same[0, row]
        stack[pl.ds((1 - core) * depth, depth)] = cross[1, row]
        block[:, row] = members_inside(stack[...])
    levels = pl.ds(pl.multiple_of(chip * 8, 8), 8)
    copies = [
        pltpu.make_async_copy(block.at[:, pl.ds(2 * i, 2)], out.at[:, pl.ds(4 * i, 2), levels, :], sems.at[i])
        for i in range(2)
    ]
    for copy in copies:
        copy.start()
    for copy in copies:
        copy.wait()


def per_device(ensemble, courant, obs_column, obs_value, obs_var):
    members, levels, rows, cells = ensemble.shape
    count = lax.axis_size("rows")
    mem = lax.axis_size("mem")
    field = jnp.transpose(ensemble, (0, 2, 1, 3))
    if not INTERPRET:
        field = pltpu.with_memory_space_constraint(field, pltpu.HBM)
    flow = jnp.transpose(courant, (0, 2, 1, 3))
    row_shape = (levels, members, cells)
    row_bytes = 4 * levels * members * cells

    def row_spec(row):
        return pl.BlockSpec((members, 1, levels, cells), lambda *_: (0, row, 0, 0))

    def relayout(which, with_courant=False):
        full = pl.BlockSpec(row_shape, lambda *_: (0, 0, 0))
        shapes = [jax.ShapeDtypeStruct(row_shape, F32)] * 2
        in_specs, out_specs, args = [row_spec(r) for r in which], [full] * 2, [field, field]
        if with_courant:
            shape = (levels + 3 * levels // 8, members, cells)
            shapes = [jax.ShapeDtypeStruct(shape, F32)] * 2
            in_specs.append(VM)
            out_specs = [pl.BlockSpec(shape, lambda *_: (0, 0, 0))] * 2
            args.append(flow)
        return pl.pallas_call(
            rows_courant_body if with_courant else rows_body,
            grid=(1,),
            out_shape=shapes,
            in_specs=in_specs,
            out_specs=out_specs,
            compiler_params=PARAMS,
            interpret=INTERPRET,
        )(*args)

    up = [(i, i + 1) for i in range(count - 1)]
    down = [(i + 1, i) for i in range(count - 1)]

    def exchange(first, last):
        return lax.ppermute(last, "rows", up), lax.ppermute(first, "rows", down)

    def swap(a, k):
        return lax.ppermute(a, "mem", [(i, i ^ k) for i in range(mem)])

    e0, e5 = relayout((0, 5))
    lo1, hi1 = exchange(e0, e5)
    e1, e4 = relayout((1, 4), True)
    lo2, hi2 = exchange(e1, e4)
    e2, e3 = relayout((2, 3))
    lo3, hi3 = exchange(e2, e3)
    lo2x, hi2x = swap(lo2, 1), swap(hi2, 1)
    coef = call(own_coefficients, (rows, 7, levels, cells), 1, nbytes=7 * row_bytes)(flow)

    f0, f1, f4, f5, g1, g2, g3, g4, h23 = call(
        stage_a, [row_shape] * 8 + [(2,) + row_shape], 9, [pltpu.VMEM(row_shape, F32)] * 2, nbytes=20 * row_bytes,
    )(lo1, e0, e1, e2, e3, e4, e5, hi1, coef)
    fm, fp, g0, g5, h1, h4, side = call(
        stage_b, [row_shape] * 6 + [(4, 7, levels, cells)], 17, nbytes=20 * row_bytes,
    )(lo2, lo2x, hi2, hi2x, lo1, e0, hi1, e5, f0, f1, f4, f5, g1, g2, g3, g4, coef)
    chips = mem // 2
    obs = obs_value.size
    *chunks, prof = call(
        stage_c, [(len(OUTER), levels // chips, members, cells)] * chips + [(members, obs)], 20,
        [pltpu.VMEM(row_shape, F32)] * 2 + [pltpu.VMEM((rows,) + row_shape, F32)],
        smem=1, nbytes=30 * row_bytes,
    )(obs_column, lo3, lo2, lo1, fm, f0, g0, g1, hi3, hi2, hi1, fp, f5, g5, g4, h1, h23, h4, coef, side)

    def along_chips(parts):
        got = {0: parts[0]}
        for k in ROUTE:
            got[k] = swap(parts[k], 2 * k)
        return shown(got)

    def shown(got):
        return {k: (got[k], swap(got[k], 1)) for k in got}

    def in_order(pairs):
        return [block for k in range(chips) for block in pairs[k]]

    far = [swap(prof, 2 * k) for k in (1, 2, 3)]
    profiles = []
    for a in [prof] + far:
        profiles += [a, swap(a, 1)]
    moved = in_order(along_chips(chunks))
    near = {0: h23, 1: swap(h23, 2), 3: swap(h23, 6)}
    onward = call(pick_body, h23.shape, 2, nbytes=4 * row_bytes)(near[1], near[3])
    near[2] = lax.ppermute(onward, "mem", [(i, i ^ (2 if i % 2 else 6)) for i in range(mem)])
    inner = in_order(shown(near))
    part = call(
        gram_body, (8 * members, 16 * members), 10,
        [pltpu.VMEM((8 * members, obs), F32), pltpu.VMEM((16 * members, obs), F32)], nbytes=1 << 18,
    )(*profiles, obs_value.T, obs_var.T)

    deep = mem
    wide = count // deep

    def shifted(a, dy, dz):
        pairs = [
            ((y * deep + z) * mem + m, (((y + dy) % wide) * deep + (z + dz[m % 2]) % deep) * mem + m)
            for y in range(wide) for z in range(deep) for m in range(mem)
        ]
        return lax.ppermute(a, ("rows", "mem"), pairs)

    got = [shifted(part, 0, dz) for dz in ((1, -1), (2, -2), (3, -3), (0, 4))]
    sum4 = call(sum4_body, part.shape, 4, nbytes=1 << 17)
    total = sum4(*got)
    if wide == 4:
        total = sum4(total, *[shifted(total, dy, (0, 0)) for dy in range(1, wide)])
    n = 8 * members
    left = call(weights_body, (n, 3 * n), 2, [pltpu.VMEM((n, n), F32)] * 2, nbytes=1 << 17)(total, swap(total, 1))
    mixed = call(
        mix_body, [(2, len(OUTER), levels // mem, members, cells)] * chips, 9, nbytes=18 * row_bytes,
    )(left, *moved)
    result = jax.ShapeDtypeStruct((members, rows, levels, cells), F32)
    anywhere = pl.BlockSpec(memory_space=pl.ANY)
    placed = pl.pallas_call(
        inner_body,
        out_shape=result,
        in_specs=[VM] * 9,
        out_specs=anywhere,
        scratch_shapes=[
            pltpu.VMEM((8, members, cells), F32),
            pltpu.VMEM((members, 2, levels, cells), F32),
            pltpu.SemaphoreType.DMA,
        ],
        compiler_params=PARAMS,
        interpret=INTERPRET,
        name="inner",
    )(left, *inner)
    for k, (same, cross) in along_chips(mixed).items():
        placed = pl.pallas_call(
            functools.partial(place_body, k),
            out_shape=result,
            in_specs=[VM, VM, anywhere],
            out_specs=anywhere,
            scratch_shapes=[
                pltpu.VMEM((8, members, cells), F32),
                pltpu.VMEM((members, len(OUTER), 8, cells), F32),
                pltpu.SemaphoreType.DMA((2,)),
            ],
            input_output_aliases={2: 0},
            compiler_params=PARAMS,
            interpret=INTERPRET,
        )(same, cross, placed)
    return jnp.transpose(placed, (0, 2, 1, 3))


def solution(mesh):
    return jax.shard_map(
        per_device,
        mesh=mesh,
        in_specs=(
            P("mem", None, "rows", None),
            P(None, None, "rows", None),
            P("rows"),
            P(None, "rows"),
            P(None, "rows"),
        ),
        out_specs=P("mem", None, "rows", None),
        check_vma=False,
    )
```

```python
import functools
import jax
import jax.numpy as jnp
from jax import lax
from jax.experimental import pallas as pl
from jax.experimental.pallas import tpu as pltpu
from jax.sharding import PartitionSpec as P

NS_ITERS = 4
DIFFUSION = 0.05
INTERPRET = False
F32 = jnp.float32
BF16 = jnp.bfloat16
HIGHEST = lax.Precision.HIGHEST
VM = pl.BlockSpec(memory_space=pltpu.VMEM)
SM = pl.BlockSpec(memory_space=pltpu.SMEM)
PARAMS = pltpu.CompilerParams(vmem_limit_bytes=16 * 2**20)
ROUTE = (1, 3, 2)
OUTER = (0, 1, 4, 5)


def call(body, outs, n_in, scratch=(), smem=0, flops=0, nbytes=0):
    single = not isinstance(outs, list)
    shapes = [jax.ShapeDtypeStruct(s, F32) for s in (outs if not single else [outs])]
    return pl.pallas_call(
        body,
        out_shape=shapes[0] if single else shapes,
        in_specs=[SM] * smem + [VM] * (n_in - smem),
        out_specs=VM if single else [VM] * len(shapes),
        scratch_shapes=list(scratch),
        cost_estimate=pl.CostEstimate(flops=flops, transcendentals=0, bytes_accessed=nbytes),
        compiler_params=PARAMS,
        interpret=INTERPRET,
    )


def members_inside(block):
    return jnp.swapaxes(block, 0, 1)


def relayout_row(src, dst):
    for tile in range(src.shape[2] // 8):
        part = pl.ds(8 * tile, 8)
        dst[part] = members_inside(src[:, 0, part, :])


def rows_body(first_ref, last_ref, first_out, last_out):
    relayout_row(first_ref, first_out)
    relayout_row(last_ref, last_out)


def rows_courant_body(first_ref, last_ref, courant, first_out, last_out):
    core = lax.rem(lax.axis_index("mem"), 2)
    levels = first_ref.shape[2]
    tiles = levels // 16
    for src, dst, row in ((first_ref, first_out, 0), (last_ref, last_out, courant.shape[1] - 1)):
        relayout_row(src, dst)
        for d in range(3):
            for tile in range(tiles):
                part = pl.ds(pl.multiple_of(8 * (core * tiles + tile), 8), 8)
                dst[levels + d * tiles + tile] = courant[d, row, part, :]


def pick_body(one, three, out):
    core = lax.rem(lax.axis_index("mem"), 2)
    for value, ref in ((0, one), (1, three)):

        @pl.when(core == value)
        def _():
            out[...] = ref[...]


def sum4_body(a, b, c, d, out):
    out[...] = (a[...] + b[...]) + (c[...] + d[...])


def coefficients(coef, slot, tile, levels, speeds, keep=None):
    shape = speeds[0].shape
    lane = lax.broadcasted_iota(jnp.int32, shape, 1)
    level = lax.broadcasted_iota(jnp.int32, shape, 0) + 8 * tile
    part = pl.ds(8 * tile if isinstance(tile, int) else pl.multiple_of(8 * tile, 8), 8)
    total = None
    for d, a in enumerate(speeds):
        low = jnp.maximum(a, 0.0) + DIFFUSION
        high = DIFFUSION - jnp.minimum(a, 0.0)
        both = low + high
        total = both if total is None else total + both
        if d == 1:
            low = jnp.where(lane == 0, 0.0, low)
            high = jnp.where(lane == shape[1] - 1, 0.0, high)
        if d == 2:
            low = jnp.where(level == 0, 0.0, low)
            high = jnp.where(level == levels - 1, 0.0, high)
        coef[slot, 2 * d, part] = low if keep is None else low * keep
        coef[slot, 2 * d + 1, part] = high if keep is None else high * keep
    center = 1.0 - total
    coef[slot, 6, part] = center if keep is None else center * keep


def own_coefficients(courant, coef):
    levels = courant.shape[2]
    for row in range(courant.shape[1]):
        for tile in range(levels // 8):
            coefficients(coef, row, tile, levels, [courant[d, row, pl.ds(8 * tile, 8), :] for d in range(3)])


def halo_coefficients(coef, halos, levels):
    core = lax.rem(lax.axis_index("mem"), 2)
    block = lax.axis_index("rows")
    inside = (block > 0, block < lax.axis_size("rows") - 1)
    tiles = levels // 16
    for side in range(2):
        keep = jnp.where(inside[side], 1.0, 0.0).astype(F32)
        for part, half in ((halos[2 * side], core), (halos[2 * side + 1], 1 - core)):
            for tile in range(tiles):
                speeds = [part[levels + d * tiles + tile] for d in range(3)]
                coefficients(coef, side, half * tiles + tile, levels, speeds, keep)


def advance_row(dst, below, here, above, coef, slot):
    levels, members, cells = dst.shape

    def level_step(z, carry):
        before, c = carry

        def k(i):
            return jnp.broadcast_to(coef[slot, i, pl.ds(z, 1), :], (members, cells))

        after = here[jnp.minimum(z + 1, levels - 1)]
        new = c * k(6)
        new += k(0) * below[z] + k(1) * above[z]
        new += k(2) * pltpu.roll(c, 1, 1) + k(3) * pltpu.roll(c, cells - 1, 1)
        new += k(4) * before + k(5) * after
        dst[z] = new
        return c, after

    first = here[0]
    lax.fori_loop(0, levels, level_step, (first, first), unroll=32)


def stage_a(lo1, e0, e1, e2, e3, e4, e5, hi1, coef, f0, f1, f4, f5, g1, g2, g3, g4, h23, f2, f3):
    e = [lo1, e0, e1, e2, e3, e4, e5, hi1]
    f = [f0, f1, f2, f3, f4, f5]
    g = [None, g1, g2, g3, g4]
    for row in range(6):
        advance_row(f[row], e[row], e[row + 1], e[row + 2], coef, row)
    for row in (1, 2, 3, 4):
        advance_row(g[row], f[row - 1], f[row], f[row + 1], coef, row)
    for row in (2, 3):
        advance_row(h23.at[row - 2], g[row - 1], g[row], g[row + 1], coef, row)


def stage_b(lo2, lo2x, hi2, hi2x, lo1, e0, hi1, e5, f0, f1, f4, f5, g1, g2, g3, g4, coef, *outs):
    fm, fp, g0, g5, h1, h4, side = outs
    halo_coefficients(side, (lo2, lo2x, hi2, hi2x), e0.shape[0])
    advance_row(fm, lo2, lo1, e0, side, 0)
    advance_row(fp, e5, hi1, hi2, side, 1)
    advance_row(g0, fm, f0, f1, coef, 0)
    advance_row(g5, f4, f5, fp, coef, 5)
    advance_row(h1, g0, g1, g2, coef, 1)
    advance_row(h4, g3, g4, g5, coef, 4)


def stage_c(obs_column, *refs):
    lo3, fm, f0, g0, g1, hi3, fp, f5, g5, g4, h1, h23, h4, coef, side = refs[:15]
    prof, full, low, high = refs[15:]
    levels, members, cells = g0.shape
    origin = lax.axis_index("rows") * (6 * cells)
    full[1] = h1[...]
    full[pl.ds(2, 2)] = h23[...]
    full[4] = h4[...]
    advance_row(low, lo3, fm, f0, side, 0)
    advance_row(full.at[0], low, g0, g1, coef, 0)
    advance_row(high, f5, fp, hi3, side, 1)
    advance_row(full.at[5], g4, g5, high, coef, 5)
    per = prof.shape[1] // levels
    lane = lax.broadcasted_iota(jnp.int32, (members, 128), 1)
    group = 128 // levels
    acc = [jnp.zeros((members, 128), F32) for _ in range(per // group)]
    for p in range(per):
        column = jnp.clip(obs_column[p] - origin, 0, 6 * cells - 1)
        row = lax.div(column, cells)
        y = column - row * cells
        tile = lax.div(y, 128)
        shift = 128 - (y - tile * 128)
        for z in range(levels):
            spot = (p % group) * levels + z
            v = full[row, z, :, pl.ds(pl.multiple_of(tile * 128, 128), 128)]
            v = pltpu.roll(v, lax.rem(shift + spot, 128), 1)
            acc[p // group] = jnp.where(lane == spot, v, acc[p // group])
    for i, a in enumerate(acc):
        prof[:, pl.ds(128 * i, 128)] = a


def emit_body(full, *chunks):
    depth = chunks[0].shape[1]
    for k, chunk in enumerate(chunks):
        chip = lax.bitwise_xor(lax.div(lax.axis_index("mem"), 2), k)
        for i, row in enumerate(OUTER):
            chunk[i] = full[row, pl.ds(chip * depth, depth)]


def flat_rows(ref):
    return jnp.concatenate([ref[pl.ds(p, 1), :] for p in range(ref.shape[0])], axis=1)


def gram_body(*refs):
    profiles, (value, var, out, stack, aug) = refs[:8], refs[8:]
    me = lax.axis_index("mem")
    members = profiles[0].shape[0]
    for k, profile in enumerate(profiles):
        mate = lax.bitwise_xor(me, k)
        stack[pl.ds(pl.multiple_of(mate * members, members), members), :] = profile[...]
    total = stack.shape[0]
    everyone = stack[...]
    center = jnp.sum(everyone, axis=0, keepdims=True) * (1.0 / total)
    variance = flat_rows(var)
    scaling = 1.0 / jnp.sqrt((total - 1.0) * variance)
    scaled = (everyone - center) * scaling
    innovation = (flat_rows(value) - center) / jnp.sqrt(variance)
    aug[pl.ds(0, total), :] = scaled
    first = lax.broadcasted_iota(jnp.int32, everyone.shape, 0) == 0
    aug[pl.ds(total, total), :] = jnp.where(first, jnp.broadcast_to(innovation, everyone.shape), 0.0)
    out[...] = lax.dot_general(
        scaled, aug[...], (((1,), (1,)), ((), ())), precision=HIGHEST, preferred_element_type=F32
    )


def transform_weights(both):
    n = both.shape[0]
    gram = both[:, :n]
    pull = both[:, n:]

    def dot(a, b):
        return jnp.dot(a, b, precision=HIGHEST, preferred_element_type=F32)

    rows = lax.broadcasted_iota(jnp.int32, (n, n), 0)
    cols = lax.broadcasted_iota(jnp.int32, (n, n), 1)
    eye = jnp.where(rows == cols, 1.0, 0.0).astype(F32)
    system = eye + gram
    squares = jnp.sum(jnp.sum(system * system, axis=1, keepdims=True), axis=0, keepdims=True)
    frobenius = jnp.sqrt(squares)
    y = system / frobenius
    z = None
    for i in range(NS_ITERS):
        factor = 0.5 * (3.0 * eye - (y if z is None else dot(z, y)))
        if i < NS_ITERS - 1:
            y = dot(y, factor)
        z = factor if z is None else dot(factor, z)
    root = z / jnp.sqrt(frobenius)
    shift = dot(root, dot(root, pull)) * (1.0 / (n - 1.0) ** 0.5)
    moved = shift[:, :1] + root
    return moved - jnp.sum(moved, axis=0, keepdims=True) * (1.0 / n) + 1.0 / n


def weights_body(own, other, lhs, w_ref, t_ref):
    me = lax.axis_index("mem")
    weights = transform_weights(own[...] + other[...])
    w_ref[...] = weights
    for k in range(8):
        q = lax.bitwise_xor(me, k)
        t_ref[pl.ds(8 * k, 8), :] = w_ref[pl.ds(pl.multiple_of(8 * q, 8), 8), :]
    w_ref[...] = t_ref[...].T
    for k in range(8):
        q = lax.bitwise_xor(me, k)
        t_ref[pl.ds(8 * k, 8), :] = w_ref[pl.ds(pl.multiple_of(8 * q, 8), 8), :]
    left = t_ref[...]
    high = left.astype(BF16).astype(F32)
    lhs[...] = jnp.concatenate([high, left - high, high], axis=1)


def mixed_levels(lhs, blocks):
    f = jnp.concatenate(blocks, axis=0)
    hi = f.astype(BF16)
    lo = (f - hi.astype(F32)).astype(BF16)
    return jnp.dot(lhs, jnp.concatenate([hi, hi, lo], axis=0), preferred_element_type=F32)


def mix_body(left, *rest):
    chunks, outs = rest[:8], rest[8:]
    lhs = left[...].astype(BF16)
    rows, depth = outs[0].shape[1], outs[0].shape[2]
    start = lax.rem(lax.axis_index("mem"), 2) * depth
    for row in range(rows):
        for z in range(depth):
            o = mixed_levels(lhs, [c[row, start + z] for c in chunks])
            for k in range(8):
                outs[k // 2][k % 2, row, z] = o[8 * k : 8 * k + 8]


def inner_body(left, *rest):
    fields, (out, stack, block, sem) = rest[:8], rest[-4:]
    members = stack.shape[1]
    lhs = left[pl.ds(0, 2 * members), :].astype(BF16)
    for row in range(2):

        def tile(t, carry):
            for z in range(8):
                o = mixed_levels(lhs, [f[row, 8 * t + z] for f in fields])
                stack[z] = o[:members]
            block[:, row, pl.ds(pl.multiple_of(8 * t, 8), 8), :] = members_inside(stack[...])
            return carry

        lax.fori_loop(0, fields[0].shape[1] // 8, tile, 0)
    copy = pltpu.make_async_copy(block, out.at[:, pl.ds(2, 2)], sem)
    copy.start()
    copy.wait()


def place_body(distances, *refs):
    pairs, (out, stack, block, sems) = refs[: 2 * len(distances)], refs[-4:]
    me = lax.axis_index("mem")
    core = lax.rem(me, 2)
    copies = []
    for n, distance in enumerate(distances):
        same, cross = pairs[2 * n], pairs[2 * n + 1]
        rows, depth = same.shape[1], same.shape[2]
        for row in range(rows):
            stack[pl.ds(core * depth, depth)] = same[0, row]
            stack[pl.ds((1 - core) * depth, depth)] = cross[1, row]
            block[n, :, row] = members_inside(stack[...])
        levels = pl.ds(pl.multiple_of(lax.bitwise_xor(lax.div(me, 2), distance) * 8, 8), 8)
        for i in range(2):
            here = block.at[n, :, pl.ds(2 * i, 2)]
            copies.append(pltpu.make_async_copy(here, out.at[:, pl.ds(4 * i, 2), levels, :], sems.at[2 * n + i]))
            copies[-1].start()
    for copy in copies:
        copy.wait()


def per_device(ensemble, courant, obs_column, obs_value, obs_var):
    members, levels, rows, cells = ensemble.shape
    count = lax.axis_size("rows")
    mem = lax.axis_size("mem")
    field = jnp.transpose(ensemble, (0, 2, 1, 3))
    if not INTERPRET:
        field = pltpu.with_memory_space_constraint(field, pltpu.HBM)
    flow = jnp.transpose(courant, (0, 2, 1, 3))
    row_shape = (levels, members, cells)
    row_bytes = 4 * levels * members * cells

    def row_spec(row):
        return pl.BlockSpec((members, 1, levels, cells), lambda *_: (0, row, 0, 0))

    def relayout(which, with_courant=False):
        full = pl.BlockSpec(row_shape, lambda *_: (0, 0, 0))
        shapes = [jax.ShapeDtypeStruct(row_shape, F32)] * 2
        in_specs, out_specs, args = [row_spec(r) for r in which], [full] * 2, [field, field]
        if with_courant:
            shape = (levels + 3 * levels // 16, members, cells)
            shapes = [jax.ShapeDtypeStruct(shape, F32)] * 2
            in_specs.append(VM)
            out_specs = [pl.BlockSpec(shape, lambda *_: (0, 0, 0))] * 2
            args.append(flow)
        return pl.pallas_call(
            rows_courant_body if with_courant else rows_body,
            grid=(1,),
            out_shape=shapes,
            in_specs=in_specs,
            out_specs=out_specs,
            compiler_params=PARAMS,
            interpret=INTERPRET,
        )(*args)

    up = [(i, i + 1) for i in range(count - 1)]
    down = [(i + 1, i) for i in range(count - 1)]

    def exchange(first, last):
        return lax.ppermute(last, "rows", up), lax.ppermute(first, "rows", down)

    def swap(a, k):
        return lax.ppermute(a, "mem", [(i, i ^ k) for i in range(mem)])

    e0, e5 = relayout((0, 5))
    lo1, hi1 = exchange(e0, e5)
    e1, e4 = relayout((1, 4), True)
    lo2, hi2 = exchange(e1, e4)
    e2, e3 = relayout((2, 3))
    lo2x, hi2x = swap(lo2, 1), swap(hi2, 1)
    coef = call(own_coefficients, (rows, 7, levels, cells), 1, nbytes=7 * row_bytes)(flow)

    f0, f1, f4, f5, g1, g2, g3, g4, h23 = call(
        stage_a, [row_shape] * 8 + [(2,) + row_shape], 9, [pltpu.VMEM(row_shape, F32)] * 2, nbytes=20 * row_bytes,
    )(lo1, e0, e1, e2, e3, e4, e5, hi1, coef)
    lo3, hi3 = exchange(f1, f4)
    fm, fp, g0, g5, h1, h4, side = call(
        stage_b, [row_shape] * 6 + [(2, 7, levels, cells)], 17, nbytes=20 * row_bytes,
    )(lo2, lo2x, hi2, hi2x, lo1, e0, hi1, e5, f0, f1, f4, f5, g1, g2, g3, g4, coef)
    chips = mem // 2
    obs = obs_value.size
    prof, full = call(
        stage_c, [(members, obs), (rows,) + row_shape], 16, [pltpu.VMEM(row_shape, F32)] * 2,
        smem=1, nbytes=30 * row_bytes,
    )(obs_column, lo3, fm, f0, g0, g1, hi3, fp, f5, g5, g4, h1, h23, h4, coef, side)
    chunks = call(emit_body, [(len(OUTER), levels // chips, members, cells)] * chips, 1, nbytes=8 * row_bytes)(full)

    def along_chips(parts):
        got = {0: parts[0]}
        for k in ROUTE:
            got[k] = swap(parts[k], 2 * k)
        return shown(got)

    def shown(got):
        return {k: (got[k], swap(got[k], 1)) for k in got}

    def in_order(pairs):
        return [block for k in range(chips) for block in pairs[k]]

    far = [swap(prof, 2 * k) for k in (1, 2, 3)]
    profiles = []
    for a in [prof] + far:
        profiles += [a, swap(a, 1)]
    moved = in_order(along_chips(chunks))
    near = {0: h23, 1: swap(h23, 2), 3: swap(h23, 6)}
    onward = call(pick_body, h23.shape, 2, nbytes=4 * row_bytes)(near[1], near[3])
    near[2] = lax.ppermute(onward, "mem", [(i, i ^ (2 if i % 2 else 6)) for i in range(mem)])
    inner = in_order(shown(near))
    part = call(
        gram_body, (8 * members, 16 * members), 10,
        [pltpu.VMEM((8 * members, obs), F32), pltpu.VMEM((16 * members, obs), F32)], nbytes=1 << 18,
    )(*profiles, obs_value.T, obs_var.T)

    deep = mem
    wide = count // deep

    def shifted(a, dy, dz):
        pairs = [
            ((y * deep + z) * mem + m, (((y + dy) % wide) * deep + (z + dz[m % 2]) % deep) * mem + m)
            for y in range(wide) for z in range(deep) for m in range(mem)
        ]
        return lax.ppermute(a, ("rows", "mem"), pairs)

    got = [shifted(part, 0, dz) for dz in ((1, -1), (2, -2), (3, -3), (0, 4))]
    sum4 = call(sum4_body, part.shape, 4, nbytes=1 << 17)
    total = sum4(*got)
    if wide == 4:
        total = sum4(total, *[shifted(total, dy, (0, 0)) for dy in range(1, wide)])
    n = 8 * members
    left = call(weights_body, (n, 3 * n), 2, [pltpu.VMEM((n, n), F32)] * 2, nbytes=1 << 17)(total, swap(total, 1))
    mixed = call(
        mix_body, [(2, len(OUTER), levels // mem, members, cells)] * chips, 9, nbytes=18 * row_bytes,
    )(left, *moved)
    result = jax.ShapeDtypeStruct((members, rows, levels, cells), F32)
    anywhere = pl.BlockSpec(memory_space=pl.ANY)
    placed = pl.pallas_call(
        inner_body,
        out_shape=result,
        in_specs=[VM] * 9,
        out_specs=anywhere,
        scratch_shapes=[
            pltpu.VMEM((8, members, cells), F32),
            pltpu.VMEM((members, 2, levels, cells), F32),
            pltpu.SemaphoreType.DMA,
        ],
        compiler_params=PARAMS,
        interpret=INTERPRET,
        name="inner",
    )(left, *inner)
    back = along_chips(mixed)
    for distances in ((0,), ROUTE):
        count = len(distances)
        placed = pl.pallas_call(
            functools.partial(place_body, distances),
            out_shape=result,
            in_specs=[VM] * (2 * count) + [anywhere],
            out_specs=anywhere,
            scratch_shapes=[
                pltpu.VMEM((8, members, cells), F32),
                pltpu.VMEM((count, members, len(OUTER), 8, cells), F32),
                pltpu.SemaphoreType.DMA((2 * count,)),
            ],
            input_output_aliases={2 * count: 0},
            compiler_params=PARAMS,
            interpret=INTERPRET,
        )(*[block for k in distances for block in back[k]], placed)
    return jnp.transpose(placed, (0, 2, 1, 3))


def solution(mesh):
    return jax.shard_map(
        per_device,
        mesh=mesh,
        in_specs=(
            P("mem", None, "rows", None),
            P(None, None, "rows", None),
            P("rows"),
            P(None, "rows"),
            P(None, "rows"),
        ),
        out_specs=P("mem", None, "rows", None),
        check_vma=False,
    )
```

```python
import functools
import jax
import jax.numpy as jnp
from jax import lax
from jax.experimental import pallas as pl
from jax.experimental.pallas import tpu as pltpu
from jax.sharding import PartitionSpec as P

NS_ITERS = 4
DIFFUSION = 0.05
INTERPRET = False
F32 = jnp.float32
BF16 = jnp.bfloat16
HIGHEST = lax.Precision.HIGHEST
VM = pl.BlockSpec(memory_space=pltpu.VMEM)
SM = pl.BlockSpec(memory_space=pltpu.SMEM)
PARAMS = pltpu.CompilerParams(vmem_limit_bytes=16 * 2**20)
ROUTE = (1, 3, 2)
OUTER = (0, 1, 4, 5)


def call(body, outs, n_in, scratch=(), smem=0, flops=0, nbytes=0):
    single = not isinstance(outs, list)
    shapes = [jax.ShapeDtypeStruct(s, F32) for s in (outs if not single else [outs])]
    return pl.pallas_call(
        body,
        out_shape=shapes[0] if single else shapes,
        in_specs=[SM] * smem + [VM] * (n_in - smem),
        out_specs=VM if single else [VM] * len(shapes),
        scratch_shapes=list(scratch),
        cost_estimate=pl.CostEstimate(flops=flops, transcendentals=0, bytes_accessed=nbytes),
        compiler_params=PARAMS,
        interpret=INTERPRET,
    )


def members_inside(block):
    return jnp.swapaxes(block, 0, 1)


def relayout_row(src, dst):
    for tile in range(src.shape[2] // 8):
        part = pl.ds(8 * tile, 8)
        dst[part] = members_inside(src[:, 0, part, :])


def by_parity(body):
    even = lax.rem(lax.axis_index("rows"), 2) == 0
    pl.when(even)(lambda: body(True))
    pl.when(jnp.logical_not(even))(lambda: body(False))


def rows_05_body(first_ref, last_ref, one, two):
    def fill(even):
        relayout_row(last_ref if even else first_ref, one)
        relayout_row(first_ref if even else last_ref, two)

    by_parity(fill)


def rows_14_body(first_ref, last_ref, courant, first_out, last_out, one, two):
    core = lax.rem(lax.axis_index("mem"), 2)
    levels = first_ref.shape[2]
    tiles = levels // 16
    relayout_row(first_ref, first_out)
    relayout_row(last_ref, last_out)

    def fill(even):
        low, high = (two, one) if even else (one, two)
        for src, dst, row in ((first_out, low, 0), (last_out, high, courant.shape[1] - 1)):
            dst[pl.ds(0, levels)] = src[...]
            for d in range(3):
                for tile in range(tiles):
                    part = pl.ds(pl.multiple_of(8 * (core * tiles + tile), 8), 8)
                    dst[levels + d * tiles + tile] = courant[d, row, part, :]

    by_parity(fill)


def rows_23_body(first_ref, last_ref, one, two, first_out, last_out, bottom, top):
    relayout_row(first_ref, first_out)
    relayout_row(last_ref, last_out)

    def fill(even):
        bottom[...] = (two if even else one)[...]
        top[...] = (one if even else two)[...]

    by_parity(fill)


def pick_body(one, three, out):
    core = lax.rem(lax.axis_index("mem"), 2)
    for value, ref in ((0, one), (1, three)):

        @pl.when(core == value)
        def _():
            out[...] = ref[...]


def sum4_body(a, b, c, d, out):
    out[...] = (a[...] + b[...]) + (c[...] + d[...])


def coefficients(coef, slot, tile, levels, speeds, keep=None):
    shape = speeds[0].shape
    lane = lax.broadcasted_iota(jnp.int32, shape, 1)
    level = lax.broadcasted_iota(jnp.int32, shape, 0) + 8 * tile
    part = pl.ds(8 * tile if isinstance(tile, int) else pl.multiple_of(8 * tile, 8), 8)
    total = None
    for d, a in enumerate(speeds):
        low = jnp.maximum(a, 0.0) + DIFFUSION
        high = DIFFUSION - jnp.minimum(a, 0.0)
        both = low + high
        total = both if total is None else total + both
        if d == 1:
            low = jnp.where(lane == 0, 0.0, low)
            high = jnp.where(lane == shape[1] - 1, 0.0, high)
        if d == 2:
            low = jnp.where(level == 0, 0.0, low)
            high = jnp.where(level == levels - 1, 0.0, high)
        coef[slot, 2 * d, part] = low if keep is None else low * keep
        coef[slot, 2 * d + 1, part] = high if keep is None else high * keep
    center = 1.0 - total
    coef[slot, 6, part] = center if keep is None else center * keep


def own_coefficients(courant, coef):
    levels = courant.shape[2]
    for row in range(courant.shape[1]):
        for tile in range(levels // 8):
            coefficients(coef, row, tile, levels, [courant[d, row, pl.ds(8 * tile, 8), :] for d in range(3)])


def halo_coefficients(coef, halos, levels):
    core = lax.rem(lax.axis_index("mem"), 2)
    block = lax.axis_index("rows")
    inside = (block > 0, block < lax.axis_size("rows") - 1)
    tiles = levels // 16
    for side in range(2):
        keep = jnp.where(inside[side], 1.0, 0.0).astype(F32)
        for part, half in ((halos[2 * side], core), (halos[2 * side + 1], 1 - core)):
            for tile in range(tiles):
                speeds = [part[levels + d * tiles + tile] for d in range(3)]
                coefficients(coef, side, half * tiles + tile, levels, speeds, keep)


def advance_row(dst, below, here, above, coef, slot):
    levels, members, cells = dst.shape

    def level_step(z, carry):
        before, c = carry

        def k(i):
            return jnp.broadcast_to(coef[slot, i, pl.ds(z, 1), :], (members, cells))

        after = here[jnp.minimum(z + 1, levels - 1)]
        new = c * k(6)
        new += k(0) * below[z] + k(1) * above[z]
        new += k(2) * pltpu.roll(c, 1, 1) + k(3) * pltpu.roll(c, cells - 1, 1)
        new += k(4) * before + k(5) * after
        dst[z] = new
        return c, after

    first = here[0]
    lax.fori_loop(0, levels, level_step, (first, first), unroll=32)


def stage_a(one, two, e0, e1, e2, e3, e4, e5, coef, *rest):
    f0, f1, f4, f5, g1, g2, g3, g4, h23, lo1, hi1, out_one, out_two, f2, f3 = rest

    def settle(even):
        lo1[...] = (two if even else one)[...]
        hi1[...] = (one if even else two)[...]

    by_parity(settle)
    e = [lo1, e0, e1, e2, e3, e4, e5, hi1]
    f = [f0, f1, f2, f3, f4, f5]
    g = [None, g1, g2, g3, g4]
    for row in range(6):
        advance_row(f[row], e[row], e[row + 1], e[row + 2], coef, row)

    def send(even):
        out_one[...] = (f4 if even else f1)[...]
        out_two[...] = (f1 if even else f4)[...]

    by_parity(send)
    for row in (1, 2, 3, 4):
        advance_row(g[row], f[row - 1], f[row], f[row + 1], coef, row)
    for row in (2, 3):
        advance_row(h23.at[row - 2], g[row - 1], g[row], g[row + 1], coef, row)


def stage_b(one, onex, two, twox, lo1, e0, hi1, e5, f0, f1, f4, f5, g1, g2, g3, g4, coef, *outs):
    fm, fp, g0, g5, h1, h4, side, lo2, hi2 = outs

    def settle(even):
        below, above = ((two, twox), (one, onex)) if even else ((one, onex), (two, twox))
        halo_coefficients(side, below + above, lo2.shape[0])
        lo2[...] = below[0][pl.ds(0, lo2.shape[0])]
        hi2[...] = above[0][pl.ds(0, hi2.shape[0])]

    by_parity(settle)
    advance_row(fm, lo2, lo1, e0, side, 0)
    advance_row(fp, e5, hi1, hi2, side, 1)
    advance_row(g0, fm, f0, f1, coef, 0)
    advance_row(g5, f4, f5, fp, coef, 5)
    advance_row(h1, g0, g1, g2, coef, 1)
    advance_row(h4, g3, g4, g5, coef, 4)


def stage_c(obs_column, *refs):
    one, two, fm, f0, g0, g1, fp, f5, g5, g4, h1, h23, h4, coef, side = refs[:15]
    prof, full, low, high, lo3, hi3 = refs[15:]

    def settle(even):
        lo3[...] = (two if even else one)[...]
        hi3[...] = (one if even else two)[...]

    by_parity(settle)
    levels, members, cells = g0.shape
    origin = lax.axis_index("rows") * (6 * cells)
    full[1] = h1[...]
    full[pl.ds(2, 2)] = h23[...]
    full[4] = h4[...]
    advance_row(low, lo3, fm, f0, side, 0)
    advance_row(full.at[0], low, g0, g1, coef, 0)
    advance_row(high, f5, fp, hi3, side, 1)
    advance_row(full.at[5], g4, g5, high, coef, 5)
    per = prof.shape[1] // levels
    lane = lax.broadcasted_iota(jnp.int32, (members, 128), 1)
    group = 128 // levels
    acc = [jnp.zeros((members, 128), F32) for _ in range(per // group)]
    for p in range(per):
        column = jnp.clip(obs_column[p] - origin, 0, 6 * cells - 1)
        row = lax.div(column, cells)
        y = column - row * cells
        tile = lax.div(y, 128)
        shift = 128 - (y - tile * 128)
        for z in range(levels):
            spot = (p % group) * levels + z
            v = full[row, z, :, pl.ds(pl.multiple_of(tile * 128, 128), 128)]
            v = pltpu.roll(v, lax.rem(shift + spot, 128), 1)
            acc[p // group] = jnp.where(lane == spot, v, acc[p // group])
    for i, a in enumerate(acc):
        prof[:, pl.ds(128 * i, 128)] = a


def emit_body(full, *chunks):
    depth = chunks[0].shape[1]
    for k, chunk in enumerate(chunks):
        chip = lax.bitwise_xor(lax.div(lax.axis_index("mem"), 2), k)
        for i, row in enumerate(OUTER):
            chunk[i] = full[row, pl.ds(chip * depth, depth)]


def flat_rows(ref):
    return jnp.concatenate([ref[pl.ds(p, 1), :] for p in range(ref.shape[0])], axis=1)


def gram_body(*refs):
    profiles, (value, var, out, stack, aug) = refs[:8], refs[8:]
    me = lax.axis_index("mem")
    members = profiles[0].shape[0]
    for k, profile in enumerate(profiles):
        mate = lax.bitwise_xor(me, k)
        stack[pl.ds(pl.multiple_of(mate * members, members), members), :] = profile[...]
    total = stack.shape[0]
    everyone = stack[...]
    center = jnp.sum(everyone, axis=0, keepdims=True) * (1.0 / total)
    variance = flat_rows(var)
    scaling = 1.0 / jnp.sqrt((total - 1.0) * variance)
    scaled = (everyone - center) * scaling
    innovation = (flat_rows(value) - center) / jnp.sqrt(variance)
    aug[pl.ds(0, total), :] = scaled
    first = lax.broadcasted_iota(jnp.int32, everyone.shape, 0) == 0
    aug[pl.ds(total, total), :] = jnp.where(first, jnp.broadcast_to(innovation, everyone.shape), 0.0)
    out[...] = lax.dot_general(
        scaled, aug[...], (((1,), (1,)), ((), ())), precision=HIGHEST, preferred_element_type=F32
    )


def transform_weights(both):
    n = both.shape[0]
    gram = both[:, :n]
    pull = both[:, n:]

    def dot(a, b):
        return jnp.dot(a, b, precision=HIGHEST, preferred_element_type=F32)

    rows = lax.broadcasted_iota(jnp.int32, (n, n), 0)
    cols = lax.broadcasted_iota(jnp.int32, (n, n), 1)
    eye = jnp.where(rows == cols, 1.0, 0.0).astype(F32)
    system = eye + gram
    squares = jnp.sum(jnp.sum(system * system, axis=1, keepdims=True), axis=0, keepdims=True)
    frobenius = jnp.sqrt(squares)
    y = system / frobenius
    z = None
    for i in range(NS_ITERS):
        factor = 0.5 * (3.0 * eye - (y if z is None else dot(z, y)))
        if i < NS_ITERS - 1:
            y = dot(y, factor)
        z = factor if z is None else dot(factor, z)
    root = z / jnp.sqrt(frobenius)
    shift = dot(root, dot(root, pull)) * (1.0 / (n - 1.0) ** 0.5)
    moved = shift[:, :1] + root
    return moved - jnp.sum(moved, axis=0, keepdims=True) * (1.0 / n) + 1.0 / n


def weights_body(own, other, lhs, w_ref, t_ref):
    me = lax.axis_index("mem")
    weights = transform_weights(own[...] + other[...])
    w_ref[...] = weights
    for k in range(8):
        q = lax.bitwise_xor(me, k)
        t_ref[pl.ds(8 * k, 8), :] = w_ref[pl.ds(pl.multiple_of(8 * q, 8), 8), :]
    w_ref[...] = t_ref[...].T
    for k in range(8):
        q = lax.bitwise_xor(me, k)
        t_ref[pl.ds(8 * k, 8), :] = w_ref[pl.ds(pl.multiple_of(8 * q, 8), 8), :]
    left = t_ref[...]
    high = left.astype(BF16).astype(F32)
    lhs[...] = jnp.concatenate([high, left - high, high], axis=1)


def mixed_levels(lhs, blocks):
    f = jnp.concatenate(blocks, axis=0)
    hi = f.astype(BF16)
    lo = (f - hi.astype(F32)).astype(BF16)
    return jnp.dot(lhs, jnp.concatenate([hi, hi, lo], axis=0), preferred_element_type=F32)


def mix_body(left, *rest):
    chunks, outs = rest[:8], rest[8:]
    lhs = left[...].astype(BF16)
    rows, depth = outs[0].shape[1], outs[0].shape[2]
    start = lax.rem(lax.axis_index("mem"), 2) * depth
    for row in range(rows):
        for z in range(depth):
            o = mixed_levels(lhs, [c[row, start + z] for c in chunks])
            for k in range(8):
                outs[k // 2][k % 2, row, z] = o[8 * k : 8 * k + 8]


def inner_body(left, *rest):
    fields, (out, stack, block, sem) = rest[:8], rest[-4:]
    members = stack.shape[1]
    lhs = left[pl.ds(0, 2 * members), :].astype(BF16)
    for row in range(2):

        def tile(t, carry):
            for z in range(8):
                o = mixed_levels(lhs, [f[row, 8 * t + z] for f in fields])
                stack[z] = o[:members]
            block[:, row, pl.ds(pl.multiple_of(8 * t, 8), 8), :] = members_inside(stack[...])
            return carry

        lax.fori_loop(0, fields[0].shape[1] // 8, tile, 0)
    copy = pltpu.make_async_copy(block, out.at[:, pl.ds(2, 2)], sem)
    copy.start()
    copy.wait()


def place_body(distances, *refs):
    pairs, (out, stack, block, sems) = refs[: 2 * len(distances)], refs[-4:]
    me = lax.axis_index("mem")
    core = lax.rem(me, 2)
    copies = []
    for n, distance in enumerate(distances):
        same, cross = pairs[2 * n], pairs[2 * n + 1]
        rows, depth = same.shape[1], same.shape[2]
        for row in range(rows):
            stack[pl.ds(core * depth, depth)] = same[0, row]
            stack[pl.ds((1 - core) * depth, depth)] = cross[1, row]
            block[n, :, row] = members_inside(stack[...])
        levels = pl.ds(pl.multiple_of(lax.bitwise_xor(lax.div(me, 2), distance) * 8, 8), 8)
        for i in range(2):
            here = block.at[n, :, pl.ds(2 * i, 2)]
            copies.append(pltpu.make_async_copy(here, out.at[:, pl.ds(4 * i, 2), levels, :], sems.at[2 * n + i]))
            copies[-1].start()
    for copy in copies:
        copy.wait()


def per_device(ensemble, courant, obs_column, obs_value, obs_var):
    members, levels, rows, cells = ensemble.shape
    count = lax.axis_size("rows")
    mem = lax.axis_size("mem")
    field = jnp.transpose(ensemble, (0, 2, 1, 3))
    if not INTERPRET:
        field = pltpu.with_memory_space_constraint(field, pltpu.HBM)
    flow = jnp.transpose(courant, (0, 2, 1, 3))
    row_shape = (levels, members, cells)
    row_bytes = 4 * levels * members * cells

    def row_spec(row):
        return pl.BlockSpec((members, 1, levels, cells), lambda *_: (0, row, 0, 0))

    def relayout(body, which, shapes, *more):
        whole = lambda shape: pl.BlockSpec(shape, lambda *_: (0, 0, 0))
        return pl.pallas_call(
            body,
            grid=(1,),
            out_shape=[jax.ShapeDtypeStruct(shape, F32) for shape in shapes],
            in_specs=[row_spec(r) for r in which] + [VM] * len(more),
            out_specs=[whole(shape) for shape in shapes],
            compiler_params=PARAMS,
            interpret=INTERPRET,
        )(field, field, *more)

    near_pairs = [(i, i ^ 1) for i in range(count)]
    far_pairs = [(i, i + 1 if i % 2 else i - 1) for i in range(1, count - 1)]

    def exchange(one, two):
        return lax.ppermute(one, "rows", near_pairs), lax.ppermute(two, "rows", far_pairs)

    def swap(a, k):
        return lax.ppermute(a, "mem", [(i, i ^ k) for i in range(mem)])

    sent = relayout(rows_05_body, (0, 5), [row_shape] * 2)
    got_1 = exchange(*sent)
    longer = (levels + 3 * levels // 16, members, cells)
    e1, e4, one, two = relayout(rows_14_body, (1, 4), [row_shape] * 2 + [longer] * 2, flow)
    one, two = exchange(one, two)
    e2, e3, e0, e5 = relayout(rows_23_body, (2, 3), [row_shape] * 4, *sent)
    onex, twox = swap(one, 1), swap(two, 1)
    coef = call(own_coefficients, (rows, 7, levels, cells), 1, nbytes=7 * row_bytes)(flow)

    f0, f1, f4, f5, g1, g2, g3, g4, h23, lo1, hi1, *sent = call(
        stage_a, [row_shape] * 8 + [(2,) + row_shape] + [row_shape] * 4, 9,
        [pltpu.VMEM(row_shape, F32)] * 2, nbytes=20 * row_bytes,
    )(*got_1, e0, e1, e2, e3, e4, e5, coef)
    got_3 = exchange(*sent)
    fm, fp, g0, g5, h1, h4, side = call(
        stage_b, [row_shape] * 6 + [(2, 7, levels, cells)], 17,
        [pltpu.VMEM(row_shape, F32)] * 2, nbytes=20 * row_bytes,
    )(one, onex, two, twox, lo1, e0, hi1, e5, f0, f1, f4, f5, g1, g2, g3, g4, coef)
    chips = mem // 2
    obs = obs_value.size
    prof, full = call(
        stage_c, [(members, obs), (rows,) + row_shape], 16, [pltpu.VMEM(row_shape, F32)] * 4,
        smem=1, nbytes=30 * row_bytes,
    )(obs_column, *got_3, fm, f0, g0, g1, fp, f5, g5, g4, h1, h23, h4, coef, side)
    chunks = call(emit_body, [(len(OUTER), levels // chips, members, cells)] * chips, 1, nbytes=8 * row_bytes)(full)

    def along_chips(parts):
        got = {0: parts[0]}
        for k in ROUTE:
            got[k] = swap(parts[k], 2 * k)
        return shown(got)

    def shown(got):
        return {k: (got[k], swap(got[k], 1)) for k in got}

    def in_order(pairs):
        return [block for k in range(chips) for block in pairs[k]]

    far = [swap(prof, 2 * k) for k in (1, 2, 3)]
    profiles = []
    for a in [prof] + far:
        profiles += [a, swap(a, 1)]
    moved = in_order(along_chips(chunks))
    near = {0: h23, 1: swap(h23, 2), 3: swap(h23, 6)}
    onward = call(pick_body, h23.shape, 2, nbytes=4 * row_bytes)(near[1], near[3])
    near[2] = lax.ppermute(onward, "mem", [(i, i ^ (2 if i % 2 else 6)) for i in range(mem)])
    inner = in_order(shown(near))
    part = call(
        gram_body, (8 * members, 16 * members), 10,
        [pltpu.VMEM((8 * members, obs), F32), pltpu.VMEM((16 * members, obs), F32)], nbytes=1 << 18,
    )(*profiles, obs_value.T, obs_var.T)

    deep = mem
    wide = count // deep

    def shifted(a, dy, dz):
        pairs = [
            ((y * deep + z) * mem + m, (((y + dy) % wide) * deep + (z + dz[m % 2]) % deep) * mem + m)
            for y in range(wide) for z in range(deep) for m in range(mem)
        ]
        return lax.ppermute(a, ("rows", "mem"), pairs)

    got = [shifted(part, 0, dz) for dz in ((1, -1), (2, -2), (3, -3), (0, 4))]
    sum4 = call(sum4_body, part.shape, 4, nbytes=1 << 17)
    total = sum4(*got)
    if wide == 4:
        total = sum4(total, *[shifted(total, dy, (0, 0)) for dy in range(1, wide)])
    n = 8 * members
    left = call(weights_body, (n, 3 * n), 2, [pltpu.VMEM((n, n), F32)] * 2, nbytes=1 << 17)(total, swap(total, 1))
    mixed = call(
        mix_body, [(2, len(OUTER), levels // mem, members, cells)] * chips, 9, nbytes=18 * row_bytes,
    )(left, *moved)
    result = jax.ShapeDtypeStruct((members, rows, levels, cells), F32)
    anywhere = pl.BlockSpec(memory_space=pl.ANY)
    placed = pl.pallas_call(
        inner_body,
        out_shape=result,
        in_specs=[VM] * 9,
        out_specs=anywhere,
        scratch_shapes=[
            pltpu.VMEM((8, members, cells), F32),
            pltpu.VMEM((members, 2, levels, cells), F32),
            pltpu.SemaphoreType.DMA,
        ],
        compiler_params=PARAMS,
        interpret=INTERPRET,
        name="inner",
    )(left, *inner)
    back = along_chips(mixed)
    for distances in ((0,), ROUTE):
        count = len(distances)
        placed = pl.pallas_call(
            functools.partial(place_body, distances),
            out_shape=result,
            in_specs=[VM] * (2 * count) + [anywhere],
            out_specs=anywhere,
            scratch_shapes=[
                pltpu.VMEM((8, members, cells), F32),
                pltpu.VMEM((count, members, len(OUTER), 8, cells), F32),
                pltpu.SemaphoreType.DMA((2 * count,)),
            ],
            input_output_aliases={2 * count: 0},
            compiler_params=PARAMS,
            interpret=INTERPRET,
        )(*[block for k in distances for block in back[k]], placed)
    return jnp.transpose(placed, (0, 2, 1, 3))


def solution(mesh):
    return jax.shard_map(
        per_device,
        mesh=mesh,
        in_specs=(
            P("mem", None, "rows", None),
            P(None, None, "rows", None),
            P("rows"),
            P(None, "rows"),
            P(None, "rows"),
        ),
        out_specs=P("mem", None, "rows", None),
        check_vma=False,
    )
```
